512 devices in a mesh: img: 8 (over y_lo, core), fsdp: 64 (over x, z, y_hi).
Axes of the slice: x: 4, y: 8 (y_hi: 2, y_lo: 4; y = y_hi * 4 + y_lo), z: 8, core: 2. Of those that a mesh axis runs over, the one named last changes fastest.
Arguments:
- text_states: bfloat16 [16384, 8192], P('fsdp')
- text_gain: float32 [8192], replicated, may hold values from 0.1 to 1.9
- vision: bfloat16 [8, 512, 8192], P('img', 'fsdp'), may hold values from -6 to 6
- q_weight: bfloat16 [8192, 4096], P('fsdp', 'img'), may hold values from -0.0625 to 0.0625
- k_weight: bfloat16 [8192, 1024], P('fsdp', 'img'), may hold values from -0.0625 to 0.0625
- v_weight: bfloat16 [8192, 1024], P('fsdp', 'img'), may hold values from -0.0625 to 0.0625
- q_gain: float32 [128], replicated, may hold values from 1 to 16
- k_gain: float32 [128], replicated, may hold values from 1 to 16
- owners: int32 [256, 4], P('fsdp'), may hold values from 0 to 7
- counts: int32 [256], P('fsdp'), may hold values from 0 to 4
- gate_value: float32 [1], replicated, may hold values from 0.3 to 1.5
Outputs:
- attended: bfloat16 [16384, 4096], P('fsdp', 'img')
The draws below stay inside these ranges and needn't reach their ends.
All inputs are finite; a program needn't handle non-finite values.
Results may differ from the reference program's by a relative error of at most 0.025.
The reference program's roundings to bfloat16 on the way (of `normed`, `queries`, `keys` and `weights`) count: a program that leaves them out, or rounds other values in their place, can miss the bound.
Values may be sent and summed in bfloat16 or wider, within the bound.
No kernel may reach another device: no remote copies, remote signals or barrier semaphores. Data moves between devices by JAX's collectives and lax.ppermute only.
A program may use at most 64 MiB of HBM per device.

```python
import math
import jax
import jax.numpy as jnp
from jax import lax

D = 8192
HD = 128
QH_DEV = 4
BLK = 64
LIST = 4
TOKENS = 16384
NBLK = 256
VIS = 512
IMAGES = 8
KVH = 8
QHEADS = 32


def draw_text_states(key, part):
    key = jax.random.fold_in(key, 13)
    first, second, third = jax.random.split(key, 3)
    base = jax.random.normal(first, (TOKENS, D), jnp.float32)
    row_scale = jnp.exp(jax.random.uniform(second, (TOKENS, 1), jnp.float32, math.log(0.5), math.log(5.0)))
    column_scale = jnp.exp(jax.random.uniform(third, (1, D), jnp.float32, math.log(0.3), math.log(3.0)))
    return (base * row_scale * column_scale).astype(jnp.bfloat16)


def gain_helper(key):
    return jnp.exp(jax.random.uniform(key, (HD,), jnp.float32, 0.0, math.log(3.0)))


def draw_q_gain(key, part):
    return gain_helper(jax.random.fold_in(key, 11))


def draw_k_gain(key, part):
    return gain_helper(jax.random.fold_in(key, 12))


def draw_counts(key, part):
    key = jax.random.fold_in(key, 14)
    first, second, third = jax.random.split(key, 3)
    values = jax.random.randint(first, (NBLK,), 0, LIST + 1, dtype=jnp.int32)
    half_blocks = NBLK // 2
    full_place = jax.random.randint(second, (), 0, half_blocks, dtype=jnp.int32)
    empty_place = half_blocks + jax.random.randint(third, (), 0, NBLK - half_blocks, dtype=jnp.int32)
    values = values.at[full_place].set(LIST)
    values = values.at[empty_place].set(0)
    return values


def plant(values, own_key, smallest, top_value):
    place = [jax.random.randint(jax.random.fold_in(own_key, axis), (), 0, length) for axis, length in enumerate(values.shape)]
    main_axis = values.shape.index(max(values.shape))
    next_to = place[:main_axis] + [(place[main_axis] + 1) % values.shape[main_axis]] + place[main_axis + 1:]
    return values.at[tuple(place)].set(smallest).at[tuple(next_to)].set(top_value)


def block_levels(stream_key, shape, pieces, low, high):
    loudness, own = 1.0, jax.random.fold_in(stream_key, 6)
    for position, parts in pieces:
        draws = jnp.exp(jax.random.uniform(jax.random.fold_in(own, position), (parts,), jnp.float32, low / len(pieces), high / len(pieces)))
        loudness = loudness * jnp.repeat(draws, shape[position] // parts).reshape([-1 if axis == position else 1 for axis in range(len(shape))])
    return loudness


def noise(own_key, extent, width, bound, shards=(), kind=jnp.bfloat16):
    level = block_levels(own_key, extent, shards, -0.22, 0.18) if shards else 1.0
    drawn = jax.random.normal(own_key, extent, jnp.float32) * width * level
    return jnp.minimum(jnp.maximum(drawn, -bound), bound).astype(kind)


def setup_inputs(seed: int = 0) -> dict:
    key_list = jax.random.split(jax.random.key(seed), 12)
    return {
        "text_states": draw_text_states(jax.random.fold_in(key_list[11], 71), 0),
        "text_gain": jnp.clip(1.0 + 0.18 * jax.random.normal(key_list[1], (D,), jnp.float32), 0.1, 1.9),
        "vision": noise(key_list[2], (IMAGES, VIS, D), 1.0, 6.0, ((0, 8), (1, 64))),
        "q_weight": noise(key_list[3], (D, QHEADS * HD), D ** -0.5, 0.0625, ((0, 64), (1, 8))),
        "k_weight": noise(key_list[4], (D, KVH * HD), D ** -0.5, 0.0625, ((0, 64), (1, 8))),
        "v_weight": noise(key_list[5], (D, KVH * HD), D ** -0.5, 0.0625, ((0, 64), (1, 8))),
        "q_gain": draw_q_gain(jax.random.fold_in(key_list[11], 71), 0),
        "k_gain": draw_k_gain(jax.random.fold_in(key_list[11], 71), 0),
        "owners": plant(jax.random.randint(key_list[8], (NBLK, LIST), 0, IMAGES), jax.random.fold_in(key_list[8], 1), 0, IMAGES - 1).astype(jnp.int32),
        "counts": draw_counts(jax.random.fold_in(key_list[11], 71), 0),
        "gate_value": jnp.clip(jax.random.uniform(key_list[10], (1,), jnp.float32, 0.3, 1.5), 0.3, 1.5),
    }


norm_epsilon = 1e-05
masked_score = -1e+30

def head_norm(values, gain):
    mean_square = lax.optimization_barrier(jnp.mean(values * values, axis=-1, keepdims=True))
    return values * lax.rsqrt(mean_square + norm_epsilon) * gain

def reference(text_states, text_gain, vision, q_weight, k_weight, v_weight, q_gain, k_gain, owners, counts, gate_value):
    text_float = text_states.astype(jnp.float32)
    normed = (text_float * lax.rsqrt(lax.optimization_barrier(jnp.mean(text_float * text_float, axis=-1, keepdims=True)) + norm_epsilon) * text_gain).astype(jnp.bfloat16)
    query_full = jnp.dot(normed, q_weight, preferred_element_type=jnp.float32)
    queries = head_norm(query_full.reshape(TOKENS, QHEADS, HD), q_gain).astype(jnp.bfloat16)
    visual = vision.reshape(IMAGES * VIS, D)
    key_full = jnp.dot(visual, k_weight, preferred_element_type=jnp.float32).reshape(IMAGES * VIS, KVH, HD)
    keys = head_norm(key_full, k_gain).astype(jnp.bfloat16)
    values = jnp.dot(visual, v_weight, preferred_element_type=jnp.float32).astype(jnp.bfloat16).reshape(IMAGES * VIS, KVH, HD)
    live_slot = jnp.arange(LIST, dtype=jnp.int32)[None, :] < counts[:, None]
    matched = (owners[:, :, None] == jnp.arange(IMAGES, dtype=jnp.int32)[None, None, :]) & live_slot[:, :, None]
    block_images = jnp.any(matched, axis=1)
    token_images = jnp.repeat(block_images, BLK, axis=0)
    key_allowed = jnp.repeat(token_images, VIS, axis=1)
    row_live = jnp.any(token_images, axis=1)
    score_scale = HD ** (-0.5)

    def one_head(head_index):
        group = head_index // QH_DEV
        query_head = queries[:, head_index, :]
        key_head = keys[:, group, :]
        value_head = values[:, group, :]
        scores = jnp.dot(query_head, key_head.T, preferred_element_type=jnp.float32) * score_scale
        scores = jnp.where(key_allowed, scores, masked_score)
        highest = lax.optimization_barrier(jnp.max(scores, axis=1, keepdims=True))
        weights = jnp.exp(scores - highest).astype(jnp.bfloat16)
        denominator = lax.optimization_barrier(jnp.sum(weights.astype(jnp.float32), axis=1, keepdims=True))
        numerator = jnp.dot(weights, value_head, preferred_element_type=jnp.float32)
        return numerator / denominator
    heads = lax.map(one_head, jnp.arange(QHEADS, dtype=jnp.int32))
    factor = jnp.where(row_live, jnp.tanh(gate_value[0]), jnp.float32(0.0))
    gated = heads * factor[None, :, None]
    return jnp.transpose(gated, (1, 0, 2)).reshape(TOKENS, QHEADS * HD).astype(jnp.bfloat16)
```

```python
import jax
import jax.numpy as jnp
from jax import lax
from jax.experimental import pallas as pl
from jax.experimental.pallas import tpu as pltpu
from jax.sharding import Mesh, PartitionSpec as P

norm_epsilon = 1e-05
masked_score = -1e30


IMG = ("yl", "co")
FSDP = ("x", "z", "yh")
SIZES = (4, 2, 4, 8, 2)


def shift(array, axis, step):
    size = lax.axis_size(axis)
    return lax.ppermute(array, axis, [(i, (i + step) % size) for i in range(size)])


def exchange(array, axes):
    return lax.all_to_all(array, axes, 0, 0, tiled=True)


def spread(array, axes):
    size = lax.axis_size(axes)
    return exchange(jnp.broadcast_to(array[None], (size, *array.shape)), axes)


def head_norm(values, gain):
    mean_square = jnp.mean(values * values, axis=-1, keepdims=True)
    return values * lax.rsqrt(mean_square + norm_epsilon) * gain


def attention_kernel(owners, counts, gate, query, q_gain, pairs, out):
    block = pl.program_id(0)
    rows, width = query.shape
    images = pairs.shape[0]
    head = q_gain.shape[1]
    heads = width // head
    slots = owners.shape[1]
    scale = head ** (-0.5)
    gain = q_gain[...]
    parts = []
    for h in range(heads):
        parts.append(head_norm(query[:, h * head : (h + 1) * head], gain).astype(jnp.bfloat16))
    queries = jnp.concatenate(parts, axis=0)
    count = counts[block]
    names = [owners[block, j] for j in range(slots)]
    scores = []
    values = []
    live = jnp.bool_(False)
    for j in range(slots):
        valid = j < count
        for i in range(j):
            valid = valid & (names[i] != names[j])
        live = live | valid
        image = jnp.clip(names[j], 0, images - 1)
        keys = pairs[image, :, :head]
        values.append(pairs[image, :, head:])
        score = (
            lax.dot_general(queries, keys, (((1,), (1,)), ((), ())), preferred_element_type=jnp.float32)
            * scale
        )
        scores.append(jnp.where(valid, score, masked_score))
    top = jnp.max(scores[0], axis=1, keepdims=True)
    for j in range(1, slots):
        top = jnp.maximum(top, jnp.max(scores[j], axis=1, keepdims=True))
    denominator = jnp.zeros_like(top)
    numerator = jnp.zeros((rows * heads, head), jnp.float32)
    for j in range(slots):
        weights = jnp.exp(scores[j] - top).astype(jnp.bfloat16)
        denominator += jnp.sum(weights.astype(jnp.float32), axis=1, keepdims=True)
        numerator += jnp.dot(weights, values[j], preferred_element_type=jnp.float32)
    factor = jnp.where(live, jnp.tanh(jnp.full((1, head), gate[0], jnp.float32)), 0.0)
    attended = (numerator / denominator * factor).astype(out.dtype)
    for h in range(heads):
        out[:, h * head : (h + 1) * head] = attended[h * rows : (h + 1) * rows]


def attention(owners, counts, gate_value, query, q_gain, pairs):
    blocks = owners.shape[0]
    tokens, width = query.shape
    rows = tokens // blocks
    scalar = pl.BlockSpec(memory_space=pltpu.SMEM)
    return pl.pallas_call(
        attention_kernel,
        grid=(blocks,),
        in_specs=[
            scalar,
            scalar,
            scalar,
            pl.BlockSpec((rows, width), lambda b: (b, 0)),
            pl.BlockSpec(q_gain.shape, lambda b: (0, 0)),
            pl.BlockSpec(pairs.shape, lambda b: (0, 0, 0)),
        ],
        out_specs=pl.BlockSpec((rows, width), lambda b: (b, 0)),
        out_shape=jax.ShapeDtypeStruct((tokens, width), jnp.bfloat16),
        name="attention",
    )(owners, counts, gate_value, query, q_gain, pairs)


def on_device(
    text_states,
    text_gain,
    vision,
    q_weight,
    k_weight,
    v_weight,
    q_gain,
    k_gain,
    owners,
    counts,
    gate_value,
):
    head = q_gain.shape[0]
    depth = q_weight.shape[0]
    tokens = vision.shape[1]
    yl, co, x, z, yh = (lax.axis_size(a) for a in IMG + FSDP)

    joined = jnp.concatenate((k_weight, v_weight, q_weight), axis=1)
    other = shift(joined, "yh", 1)
    both = jnp.where(
        lax.axis_index("yh") == 0,
        jnp.concatenate((joined, other), axis=0),
        jnp.concatenate((other, joined), axis=0),
    )
    q_full = lax.all_gather(both[:, 2 * head :], ("x", "z"), axis=0, tiled=True)
    pair_weight = spread(both[:, : 2 * head], "x").reshape(x * yh * depth, 2 * head)

    span = yh * depth
    columns = vision.reshape(tokens, x, z, span).transpose(2, 0, 1, 3).reshape(z, tokens, x * span)
    columns = jnp.broadcast_to(columns[None], (yl, *columns.shape)).reshape(yl * z, tokens, x * span)
    here = exchange(columns, ("yl", "z"))
    there = shift(here, "co", 1)
    visual = jnp.concatenate((here, there), axis=0).reshape(2 * yl * z * tokens, x * span)
    partial = jnp.dot(visual, pair_weight, preferred_element_type=jnp.float32)
    partial = partial.reshape(2 * yl, z, tokens, 2 * head).transpose(1, 0, 2, 3)
    full = jnp.sum(exchange(partial, "z"), axis=0)
    full = full.reshape(2, yl, tokens, 2 * head)
    full = jnp.where(lax.axis_index("co") == 0, full, full[::-1]).transpose(1, 0, 2, 3)
    keys = head_norm(full[..., :head], k_gain).astype(jnp.bfloat16)
    values = full[..., head:].astype(jnp.bfloat16)
    pair = jnp.concatenate((keys, values), axis=-1).reshape(yl * co, tokens, 2 * head)

    own = spread(pair, ("z", "yh")).transpose(1, 0, 2, 3).reshape(yl * co, z * yh * tokens, 2 * head)
    after = shift(own, "x", 1)
    before = shift(own, "x", -1)
    half = yl * co // 2
    low = shift(after[:half], "x", 1)
    high = shift(before[half:], "x", -1)
    across = jnp.concatenate((low, high), axis=0)
    pairs = jnp.concatenate((own, after, before, across), axis=1)

    text_float = text_states.astype(jnp.float32)
    normed = (
        text_float
        * lax.rsqrt(jnp.mean(text_float * text_float, axis=-1, keepdims=True) + norm_epsilon)
        * text_gain
    ).astype(jnp.bfloat16)
    query = jnp.dot(normed, q_full, preferred_element_type=jnp.float32)
    return attention(owners, counts, gate_value, query, q_gain[None], pairs)


def solution(mesh):
    fine = Mesh(mesh.devices.reshape(SIZES), IMG + FSDP)
    in_specs = (
        P(FSDP, None),
        P(),
        P(IMG, FSDP, None),
        P(FSDP, IMG),
        P(FSDP, IMG),
        P(FSDP, IMG),
        P(),
        P(),
        P(FSDP, None),
        P(FSDP),
        P(),
    )
    return jax.shard_map(
        on_device, mesh=fine, in_specs=in_specs, out_specs=P(FSDP, IMG), check_vma=False
    )
```

```python
import functools

import jax
import jax.numpy as jnp
from jax import lax
from jax.experimental import pallas as pl
from jax.experimental.pallas import tpu as pltpu
from jax.sharding import Mesh, PartitionSpec as P

norm_epsilon = 1e-05
masked_score = -1e30


IMG = ("yl", "co")
FSDP = ("x", "z", "yh")
SIZES = (4, 2, 4, 8, 2)


def shift(array, axis, step):
    size = lax.axis_size(axis)
    return lax.ppermute(array, axis, [(i, (i + step) % size) for i in range(size)])


def exchange(array, axes):
    return lax.all_to_all(array, axes, 0, 0, tiled=True)


def spread(array, axes):
    size = lax.axis_size(axes)
    return exchange(jnp.broadcast_to(array[None], (size, *array.shape)), axes)


def head_norm(values, gain):
    mean_square = jnp.mean(values * values, axis=-1, keepdims=True)
    return values * lax.rsqrt(mean_square + norm_epsilon) * gain


def whole(shape):
    return pl.BlockSpec(shape, lambda *_: (0,) * len(shape))


scalar = pl.BlockSpec(memory_space=pltpu.SMEM)


def half_kernel(choice, states, gain, out):
    wide = states[...].astype(jnp.float32)
    mean_square = jnp.mean(wide * wide, axis=-1, keepdims=True)
    scale = lax.rsqrt(mean_square + norm_epsilon)
    pair = choice[1] == 0
    depth = 128
    for j in range(out.shape[1] // depth):
        low = slice(2 * j * depth, (2 * j + 1) * depth)
        high = slice((2 * j + 1) * depth, (2 * j + 2) * depth)
        kept = jnp.where(pair, wide[:, low], wide[:, high])
        kept_gain = jnp.where(pair, gain[:, low], gain[:, high])
        out[:, j * depth : (j + 1) * depth] = (kept * scale * kept_gain).astype(out.dtype)


def half_rows(states, gain, choice, steps, rows):
    width = states.shape[1]
    return pl.pallas_call(
        half_kernel,
        grid_spec=pltpu.PrefetchScalarGridSpec(
            num_scalar_prefetch=1,
            grid=(steps,),
            in_specs=[
                pl.BlockSpec((rows, width), lambda i, c: (c[0] + i, 0)),
                pl.BlockSpec((1, width), lambda i, c: (0, 0)),
            ],
            out_specs=pl.BlockSpec((rows, width // 2), lambda i, c: (i, 0)),
        ),
        out_shape=jax.ShapeDtypeStruct((steps * rows, width // 2), jnp.bfloat16),
        name="half_rows",
    )(choice, states, gain)


def columns_kernel(x, vision, out):
    copies, z, tokens, width = out.shape
    span = width // x
    for c in range(copies):
        for k in range(z):
            for j in range(x):
                start = (j * z + k) * span
                out[c, k, :, j * span : (j + 1) * span] = vision[:, start : start + span]


def columns_of(vision, copies, x, z):
    tokens, width = vision.shape
    shape = (copies, z, tokens, width // z)
    return pl.pallas_call(
        functools.partial(columns_kernel, x),
        in_specs=[whole(vision.shape)],
        out_specs=whole(shape),
        grid=(1,),
        out_shape=jax.ShapeDtypeStruct(shape, vision.dtype),
        name="columns",
    )(vision)


def partial_kernel(here, there, weight, out):
    z, cores, yl, tokens, width = out.shape
    for c, part in enumerate((here, there)):
        product = jnp.dot(part[...], weight[...], preferred_element_type=jnp.float32)
        for a in range(yl):
            for k in range(z):
                row = (a * z + k) * tokens
                out[k, c, a] = product[row : row + tokens]


def partial_sums(here, there, weight, z, yl, tokens):
    shape = (z, 2, yl, tokens, weight.shape[1])
    return pl.pallas_call(
        partial_kernel,
        in_specs=[whole(here.shape), whole(there.shape), whole(weight.shape)],
        out_specs=whole(shape),
        grid=(1,),
        out_shape=jax.ShapeDtypeStruct(shape, jnp.float32),
        name="partial_sums",
    )(here, there, weight)


def pair_kernel(odd, parts, k_gain, out):
    sources, cores, yl, tokens, width = parts.shape
    head = width // 2
    copies = out.shape[0]
    swap = odd[0] != 0
    total = parts[0]
    for s in range(1, sources):
        total = total + parts[s]
    rows = jnp.concatenate([total[c, a] for c in range(cores) for a in range(yl)], axis=0)
    keys = head_norm(rows[:, :head], k_gain[...]).astype(out.dtype)
    values = rows[:, head:].astype(out.dtype)
    half = yl * tokens
    for a in range(yl):
        near = slice(a * tokens, (a + 1) * tokens)
        far = slice(half + a * tokens, half + (a + 1) * tokens)
        for piece, lanes in ((keys, slice(0, head)), (values, slice(head, width))):
            even_core = jnp.where(swap, piece[far], piece[near])
            odd_core = jnp.where(swap, piece[near], piece[far])
            for c in range(copies):
                out[c, 2 * a, :, lanes] = even_core
                out[c, 2 * a + 1, :, lanes] = odd_core


def pairs_of(odd, parts, k_gain, copies):
    sources, cores, yl, tokens, width = parts.shape
    shape = (copies, cores * yl, tokens, width)
    return pl.pallas_call(
        pair_kernel,
        in_specs=[scalar, whole(parts.shape), whole(k_gain.shape)],
        out_specs=whole(shape),
        grid=(1,),
        out_shape=jax.ShapeDtypeStruct(shape, jnp.bfloat16),
        name="key_value_pairs",
    )(odd, parts, k_gain)


def attention_kernel(owners, counts, gate, query, q_gain, own, after, before, low, high, out):
    block = pl.program_id(0)
    rows, width = query.shape
    images = own.shape[0]
    half = low.shape[0]
    head = q_gain.shape[1]
    heads = width // head
    slots = owners.shape[1]
    scale = head ** (-0.5)
    gain = q_gain[...]
    parts = []
    for h in range(heads):
        parts.append(head_norm(query[:, h * head : (h + 1) * head], gain).astype(jnp.bfloat16))
    queries = jnp.concatenate(parts, axis=0)
    count = counts[block]
    names = [owners[block, j] for j in range(slots)]
    scores = []
    values = []
    live = jnp.bool_(False)
    for j in range(slots):
        valid = j < count
        for i in range(j):
            valid = valid & (names[i] != names[j])
        live = live | valid
        image = jnp.clip(names[j], 0, images - 1)
        lower = jnp.minimum(image, half - 1)
        upper = jnp.maximum(image - half, 0)
        across = jnp.where(image < half, low[lower], high[upper])
        pairs = jnp.concatenate((own[image], after[image], before[image], across), axis=0)
        values.append(pairs[:, head:])
        score = (
            lax.dot_general(
                queries, pairs[:, :head], (((1,), (1,)), ((), ())), preferred_element_type=jnp.float32
            )
            * scale
        )
        scores.append(jnp.where(valid, score, masked_score))
    top = jnp.max(scores[0], axis=1, keepdims=True)
    for j in range(1, slots):
        top = jnp.maximum(top, jnp.max(scores[j], axis=1, keepdims=True))
    denominator = jnp.zeros_like(top)
    numerator = jnp.zeros((rows * heads, head), jnp.float32)
    for j in range(slots):
        weights = jnp.exp(scores[j] - top).astype(jnp.bfloat16)
        denominator += jnp.sum(weights.astype(jnp.float32), axis=1, keepdims=True)
        numerator += jnp.dot(weights, values[j], preferred_element_type=jnp.float32)
    factor = jnp.where(live, jnp.tanh(jnp.full((1, head), gate[0], jnp.float32)), 0.0)
    attended = (numerator / denominator * factor).astype(out.dtype)
    for h in range(heads):
        out[:, h * head : (h + 1) * head] = attended[h * rows : (h + 1) * rows]


def attention(owners, counts, gate_value, query, q_gain, pieces):
    blocks = owners.shape[0]
    tokens, width = query.shape
    rows = tokens // blocks
    return pl.pallas_call(
        attention_kernel,
        grid=(blocks,),
        in_specs=[
            scalar,
            scalar,
            scalar,
            pl.BlockSpec((rows, width), lambda b: (b, 0)),
            whole(q_gain.shape),
            *(whole(p.shape) for p in pieces),
        ],
        out_specs=pl.BlockSpec((rows, width), lambda b: (b, 0)),
        out_shape=jax.ShapeDtypeStruct((tokens, width), jnp.bfloat16),
        name="attention",
    )(owners, counts, gate_value, query, q_gain, *pieces)


def on_device(
    text_states,
    text_gain,
    vision,
    q_weight,
    k_weight,
    v_weight,
    q_gain,
    k_gain,
    owners,
    counts,
    gate_value,
):
    head = q_gain.shape[0]
    depth = q_weight.shape[0]
    tokens = vision.shape[1]
    rows = text_states.shape[0]
    width = text_states.shape[1]
    yl, co, x, z, yh = (lax.axis_size(a) for a in IMG + FSDP)
    first = lax.axis_index("yh") == 0
    even = lax.axis_index("co") == 0

    q_half = lax.all_gather(q_weight, ("x", "z"), axis=0, tiled=True)

    part = rows // (yl * co)
    place = lax.axis_index("co") * yl + lax.axis_index("yl")
    mine = lax.axis_index("yh")
    sent = half_rows(text_states, text_gain[None], jnp.stack((place, 1 - mine)).astype(jnp.int32), 1, part)
    guest = spread(shift(sent, "yh", 1), "yl").reshape(yl * part, width // yh)
    guest_other = shift(guest, "co", 1)

    joined = jnp.concatenate((k_weight, v_weight), axis=1)
    other = shift(joined, "yh", 1)
    both = jnp.where(
        first,
        jnp.concatenate((joined, other), axis=0),
        jnp.concatenate((other, joined), axis=0),
    )
    pair_weight = spread(both, "x").reshape(x * yh * depth, 2 * head)

    columns = columns_of(vision.reshape(tokens, width), yl, x, z)
    here = exchange(columns.reshape(yl * z, tokens, width // z), ("yl", "z"))
    there = shift(here, "co", 1)
    partial = partial_sums(
        here.reshape(yl * z * tokens, width // z),
        there.reshape(yl * z * tokens, width // z),
        pair_weight,
        z,
        yl,
        tokens,
    )
    odd = lax.axis_index("co").astype(jnp.int32)[None]
    pair = pairs_of(odd, exchange(partial, "z"), k_gain[None], z * yh)

    own = exchange(pair, ("z", "yh")).transpose(1, 0, 2, 3).reshape(yl * co, z * yh * tokens, 2 * head)
    after = shift(own, "x", 1)
    before = shift(own, "x", -1)
    half = yl * co // 2
    low = shift(after[:half], "x", 1)
    high = shift(before[half:], "x", -1)

    guest_query = jnp.concatenate(
        (
            jnp.dot(guest, q_half, preferred_element_type=jnp.float32),
            jnp.dot(guest_other, q_half, preferred_element_type=jnp.float32),
        ),
        axis=0,
    )
    text_half = half_rows(text_states, text_gain[None], jnp.stack((0 * mine, mine)).astype(jnp.int32), yl * co, part)
    query = jnp.dot(text_half, q_half, preferred_element_type=jnp.float32)
    back = shift(guest_query, "yh", 1)
    middle = rows // 2
    query += jnp.where(even, back, jnp.concatenate((back[middle:], back[:middle]), axis=0))
    return attention(owners, counts, gate_value, query, q_gain[None], (own, after, before, low, high))


def solution(mesh):
    fine = Mesh(mesh.devices.reshape(SIZES), IMG + FSDP)
    in_specs = (
        P(FSDP, None),
        P(),
        P(IMG, FSDP, None),
        P(FSDP, IMG),
        P(FSDP, IMG),
        P(FSDP, IMG),
        P(),
        P(),
        P(FSDP, None),
        P(FSDP),
        P(),
    )
    return jax.shard_map(
        on_device, mesh=fine, in_specs=in_specs, out_specs=P(FSDP, IMG), check_vma=False
    )
```

```python
import functools

import jax
import jax.numpy as jnp
from jax import lax
from jax.experimental import pallas as pl
from jax.experimental.pallas import tpu as pltpu
from jax.sharding import Mesh, PartitionSpec as P


norm_epsilon = 1e-05
masked_score = -1e30


IMG = ("yl", "co")
FSDP = ("x", "z", "yh")
SIZES = (4, 2, 4, 8, 2)


def shift(array, axis, step):
    size = lax.axis_size(axis)
    return lax.ppermute(array, axis, [(i, (i + step) % size) for i in range(size)])


def exchange(array, axes):
    return lax.all_to_all(array, axes, 0, 0, tiled=True)


def head_norm(values, gain):
    mean_square = jnp.mean(values * values, axis=-1, keepdims=True)
    return values * lax.rsqrt(mean_square + norm_epsilon) * gain


def whole(shape):
    return pl.BlockSpec(shape, lambda *_: (0,) * len(shape))


scalar = pl.BlockSpec(memory_space=pltpu.SMEM)


def half_kernel(choice, states, gain, *rest):
    out = rest[-1]
    rows, width = states.shape
    depth = 128
    squares = jnp.zeros((rows, depth), jnp.float32)
    for j in range(width // depth):
        wide = states[:, j * depth : (j + 1) * depth].astype(jnp.float32)
        squares += wide * wide
    scale = lax.rsqrt(jnp.sum(squares, axis=-1, keepdims=True) / width + norm_epsilon)
    pair = choice[1] == 0
    for j in range(out.shape[1] // depth):
        low = slice(2 * j * depth, (2 * j + 1) * depth)
        high = slice((2 * j + 1) * depth, (2 * j + 2) * depth)
        kept = jnp.where(pair, states[:, low], states[:, high]).astype(jnp.float32)
        kept_gain = jnp.where(pair, gain[:, low], gain[:, high])
        out[:, j * depth : (j + 1) * depth] = (kept * scale * kept_gain).astype(out.dtype)


def half_rows(states, gain, choice, steps, rows, blocks=None, base=None, first=0):
    width = states.shape[1]
    blocks = blocks or steps
    held = () if base is None else (base,)
    return pl.pallas_call(
        half_kernel,
        grid_spec=pltpu.PrefetchScalarGridSpec(
            num_scalar_prefetch=1,
            grid=(steps,),
            in_specs=[
                pl.BlockSpec((rows, width), lambda i, c: (c[0] + first + i, 0)),
                pl.BlockSpec((1, width), lambda i, c: (0, 0)),
                *(pl.BlockSpec(memory_space=pl.ANY) for _ in held),
            ],
            out_specs=pl.BlockSpec((rows, width // 2), lambda i, c: (first + i, 0)),
        ),
        out_shape=jax.ShapeDtypeStruct((blocks * rows, width // 2), jnp.bfloat16),
        input_output_aliases={3: 0} if held else {},
        name="half_rows",
    )(choice, states, gain, *held)


def columns_kernel(x, vision, out):
    copies, z, _, width = out.shape
    span = width // x
    for c in range(copies):
        for k in range(z):
            for j in range(x):
                start = (j * z + k) * span
                out[c, k, :, j * span : (j + 1) * span] = vision[:, start : start + span]


def columns_of(vision, copies, x, z):
    tokens, width = vision.shape
    shape = (copies, z, tokens, width // z)
    return pl.pallas_call(
        functools.partial(columns_kernel, x),
        in_specs=[whole(vision.shape)],
        out_specs=whole(shape),
        grid=(1,),
        out_shape=jax.ShapeDtypeStruct(shape, vision.dtype),
        name="columns",
    )(vision)


def partial_kernel(spot, here, there, *rest):
    *weights, out = rest
    z, _, yl, tokens, width = out.shape
    x = len(weights)
    span = weights[0].shape[0]
    for c, part in enumerate((here, there)):
        product = jnp.zeros((part.shape[0], width), jnp.float32)
        for k, weight in enumerate(weights):
            start = pl.multiple_of(lax.rem(spot[0] + x - k, x) * span, span)
            product += jnp.dot(
                part[:, pl.ds(start, span)], weight[...], preferred_element_type=jnp.float32
            )
        for a in range(yl):
            for k in range(z):
                row = (a * z + k) * tokens
                out[k, c, a] = product[row : row + tokens]


def partial_sums(here, there, spot, weights, z, yl, tokens):
    shape = (z, 2, yl, tokens, weights[0].shape[1])
    return pl.pallas_call(
        partial_kernel,
        in_specs=[scalar, whole(here.shape), whole(there.shape), *(whole(w.shape) for w in weights)],
        out_specs=whole(shape),
        grid=(1,),
        out_shape=jax.ShapeDtypeStruct(shape, jnp.float32),
        name="partial_sums",
    )(spot, here, there, *weights)


def pair_kernel(odd, parts, k_gain, out):
    sources, cores, yl, tokens, width = parts.shape
    head = width // 2
    copies = out.shape[0]
    swap = odd[0] != 0
    total = parts[0]
    for s in range(1, sources):
        total = total + parts[s]
    rows = jnp.concatenate([total[c, a] for c in range(cores) for a in range(yl)], axis=0)
    keys = head_norm(rows[:, :head], k_gain[...]).astype(out.dtype)
    values = rows[:, head:].astype(out.dtype)
    half = yl * tokens
    for a in range(yl):
        near = slice(a * tokens, (a + 1) * tokens)
        far = slice(half + a * tokens, half + (a + 1) * tokens)
        for piece, lanes in ((keys, slice(0, head)), (values, slice(head, width))):
            even_core = jnp.where(swap, piece[far], piece[near])
            odd_core = jnp.where(swap, piece[near], piece[far])
            for c in range(copies):
                out[c, 2 * a, :, lanes] = even_core
                out[c, 2 * a + 1, :, lanes] = odd_core


def pairs_of(odd, parts, k_gain, copies):
    _, cores, yl, tokens, width = parts.shape
    shape = (copies, cores * yl, tokens, width)
    return pl.pallas_call(
        pair_kernel,
        in_specs=[scalar, whole(parts.shape), whole(k_gain.shape)],
        out_specs=whole(shape),
        grid=(1,),
        out_shape=jax.ShapeDtypeStruct(shape, jnp.bfloat16),
        name="key_value_pairs",
    )(odd, parts, k_gain)


def attention_kernel(
    part, yl, where, owners, counts, gate, query, back, q_gain, own, after, before, low, high, out
):
    block = pl.program_id(0)
    rows, width = query.shape
    images = own.shape[0]
    half = low.shape[0]
    head = q_gain.shape[1]
    heads = width // head
    slots = owners.shape[1]
    scale = head ** (-0.5)
    gain = q_gain[...]
    shares = []
    for j in range(rows // part):
        index = block * (rows // part) + j
        core = lax.rem(index // yl + where[1], 2)
        near = lax.rem(where[0] + yl - lax.rem(index, yl), yl)
        shares.append(back[pl.ds(pl.multiple_of((core * yl + near) * part, part), part), :])
    total = query[...] + jnp.concatenate(shares, axis=0)
    parts = []
    for h in range(heads):
        parts.append(head_norm(total[:, h * head : (h + 1) * head], gain).astype(jnp.bfloat16))
    queries = jnp.concatenate(parts, axis=0)
    count = counts[block]
    names = [owners[block, j] for j in range(slots)]
    scores = []
    values = []
    live = jnp.bool_(False)
    for j in range(slots):
        valid = j < count
        for i in range(j):
            valid = valid & (names[i] != names[j])
        live = live | valid
        image = jnp.clip(names[j], 0, images - 1)
        lower = jnp.minimum(image, half - 1)
        upper = jnp.maximum(image - half, 0)
        across = jnp.where(image < half, low[lower], high[upper])
        pairs = jnp.concatenate((own[image], after[image], before[image], across), axis=0)
        values.append(pairs[:, head:])
        score = (
            lax.dot_general(
                queries, pairs[:, :head], (((1,), (1,)), ((), ())), preferred_element_type=jnp.float32
            )
            * scale
        )
        scores.append(jnp.where(valid, score, masked_score))
    top = jnp.max(scores[0], axis=1, keepdims=True)
    for j in range(1, slots):
        top = jnp.maximum(top, jnp.max(scores[j], axis=1, keepdims=True))
    denominator = jnp.zeros_like(top)
    numerator = jnp.zeros((rows * heads, head), jnp.float32)
    for j in range(slots):
        weights = jnp.exp(scores[j] - top).astype(jnp.bfloat16)
        denominator += jnp.sum(weights.astype(jnp.float32), axis=1, keepdims=True)
        numerator += jnp.dot(weights, values[j], preferred_element_type=jnp.float32)
    factor = jnp.where(live, jnp.tanh(jnp.full((1, head), gate[0], jnp.float32)), 0.0)
    attended = (numerator / denominator * factor).astype(out.dtype)
    for h in range(heads):
        out[:, h * head : (h + 1) * head] = attended[h * rows : (h + 1) * rows]


def attention(where, owners, counts, gate_value, query, back, q_gain, pieces, part, yl):
    blocks = owners.shape[0]
    tokens, width = query.shape
    rows = tokens // blocks
    return pl.pallas_call(
        functools.partial(attention_kernel, part, yl),
        grid=(blocks,),
        in_specs=[
            *(scalar,) * 4,
            pl.BlockSpec((rows, width), lambda b: (b, 0)),
            whole(back.shape),
            whole(q_gain.shape),
            *(whole(p.shape) for p in pieces),
        ],
        out_specs=pl.BlockSpec((rows, width), lambda b: (b, 0)),
        out_shape=jax.ShapeDtypeStruct((tokens, width), jnp.bfloat16),
        name="attention",
    )(where, owners, counts, gate_value, query, back, q_gain, *pieces)


def on_device(
    text_states,
    text_gain,
    vision,
    q_weight,
    k_weight,
    v_weight,
    q_gain,
    k_gain,
    owners,
    counts,
    gate_value,
):
    head = q_gain.shape[0]
    tokens = vision.shape[1]
    rows = text_states.shape[0]
    width = text_states.shape[1]
    yl, co, x, z, yh = (lax.axis_size(a) for a in IMG + FSDP)
    first = lax.axis_index("yh") == 0

    q_half = lax.all_gather(q_weight, ("x", "z"), axis=0, tiled=True)

    columns = columns_of(vision.reshape(tokens, width), yl, x, z)
    here = exchange(columns.reshape(yl * z, tokens, width // z), ("yl", "z"))

    joined = jnp.concatenate((k_weight, v_weight), axis=1)
    other = shift(joined, "yh", 1)
    both = jnp.where(
        first,
        jnp.concatenate((joined, other), axis=0),
        jnp.concatenate((other, joined), axis=0),
    )
    pair_weight = (both, *(shift(both, "x", k) for k in range(1, x)))

    part = rows // (yl * co)
    place = lax.axis_index("co") * yl + lax.axis_index("yl")
    mine = lax.axis_index("yh")
    gain = text_gain[None]
    sent = half_rows(text_states, gain, jnp.stack((place, 1 - mine)).astype(jnp.int32), 1, part)
    came = [
        lax.ppermute(
            sent,
            ("yl", "yh"),
            [(a * yh + h, (a + k) % yl * yh + 1 - h) for a in range(yl) for h in range(yh)],
        )
        for k in range(yl)
    ]
    guest = jnp.concatenate(came, axis=0)
    guest_other = shift(guest, "co", 1)
    text_half = None
    choice = jnp.stack((0 * mine, mine)).astype(jnp.int32)
    pieces = 4
    blocks = yl * co
    for k in range(pieces):
        steps = blocks // pieces
        text_half = half_rows(text_states, gain, choice, steps, part, blocks, text_half, k * steps)

    there = shift(here, "co", 1)
    partial = partial_sums(
        here.reshape(yl * z * tokens, width // z),
        there.reshape(yl * z * tokens, width // z),
        lax.axis_index("x").astype(jnp.int32)[None],
        pair_weight,
        z,
        yl,
        tokens,
    )
    parts = exchange(partial, "z")
    odd = lax.axis_index("co").astype(jnp.int32)[None]
    pair = pairs_of(odd, parts, k_gain[None], z * yh)
    own = exchange(pair, ("z", "yh"))
    own = own.transpose(1, 0, 2, 3).reshape(yl * co, z * yh * tokens, 2 * head)
    after = shift(own, "x", 1)
    before = shift(own, "x", -1)
    half = yl * co // 2
    low = shift(after[:half], "x", 1)
    high = shift(before[half:], "x", -1)

    guest_query = jnp.concatenate(
        (
            jnp.dot(guest, q_half, preferred_element_type=jnp.float32),
            jnp.dot(guest_other, q_half, preferred_element_type=jnp.float32),
        ),
        axis=0,
    )
    back = shift(guest_query, "yh", 1)
    query = jnp.dot(text_half, q_half, preferred_element_type=jnp.float32)
    where = jnp.stack((lax.axis_index("yl"), lax.axis_index("co"))).astype(jnp.int32)
    return attention(
        where,
        owners,
        counts,
        gate_value,
        query,
        back,
        q_gain[None],
        (own, after, before, low, high),
        part,
        yl,
    )


def solution(mesh):
    fine = Mesh(mesh.devices.reshape(SIZES), IMG + FSDP)
    in_specs = (
        P(FSDP, None),
        P(),
        P(IMG, FSDP, None),
        P(FSDP, IMG),
        P(FSDP, IMG),
        P(FSDP, IMG),
        P(),
        P(),
        P(FSDP, None),
        P(FSDP),
        P(),
    )
    return jax.shard_map(
        on_device, mesh=fine, in_specs=in_specs, out_specs=P(FSDP, IMG), check_vma=False
    )
```

```python
import functools

import jax
import jax.numpy as jnp
from jax import lax
from jax.experimental import pallas as pl
from jax.experimental.pallas import tpu as pltpu
from jax.sharding import Mesh, PartitionSpec as P


norm_epsilon = 1e-05
masked_score = -1e30


IMG = ("yl", "co")
FSDP = ("x", "z", "yh")
SIZES = (4, 2, 4, 8, 2)


def shift(array, axis, step):
    size = lax.axis_size(axis)
    return lax.ppermute(array, axis, [(i, (i + step) % size) for i in range(size)])


def exchange(array, axes):
    return lax.all_to_all(array, axes, 0, 0, tiled=True)


def head_norm(values, gain):
    mean_square = jnp.mean(values * values, axis=-1, keepdims=True)
    return values * lax.rsqrt(mean_square + norm_epsilon) * gain


def whole(shape):
    return pl.BlockSpec(shape, lambda *_: (0,) * len(shape))


scalar = pl.BlockSpec(memory_space=pltpu.SMEM)


def half_kernel(choice, states, gain, *rest):
    outs = rest[1:]
    rows, width = states.shape
    depth = 128
    squares = jnp.zeros((rows, depth), jnp.float32)
    for j in range(width // depth):
        wide = states[:, j * depth : (j + 1) * depth].astype(jnp.float32)
        squares += wide * wide
    scale = lax.rsqrt(jnp.sum(squares, axis=-1, keepdims=True) / width + norm_epsilon)
    pair = choice[1] == 0
    for j in range(width // depth // 2):
        low = slice(2 * j * depth, (2 * j + 1) * depth)
        high = slice((2 * j + 1) * depth, (2 * j + 2) * depth)
        blocks = [
            (states[:, at].astype(jnp.float32) * scale * gain[:, at]).astype(jnp.bfloat16)
            for at in (low, high)
        ]
        lanes = slice(j * depth, (j + 1) * depth)
        outs[0][:, lanes] = jnp.where(pair, blocks[0], blocks[1])
        if len(outs) > 1:
            outs[1][:, lanes] = jnp.where(pair, blocks[1], blocks[0])


def half_rows(states, gain, choice, base):
    total, width = states.shape
    rows = 32
    steps = total // 2 // rows
    held = () if base is None else (base,)
    place = pl.BlockSpec((rows, width // 2), lambda i, c: (c[0] * steps + i, 0))
    shapes = [jax.ShapeDtypeStruct((total, width // 2), jnp.bfloat16)]
    places = [place]
    if base is None:
        held = (gain,)
        shapes.append(jax.ShapeDtypeStruct((total // 2, width // 2), jnp.bfloat16))
        places.append(pl.BlockSpec((rows, width // 2), lambda i, c: (i, 0)))
    return pl.pallas_call(
        half_kernel,
        grid_spec=pltpu.PrefetchScalarGridSpec(
            num_scalar_prefetch=1,
            grid=(steps,),
            in_specs=[
                pl.BlockSpec((rows, width), lambda i, c: (c[0] * steps + i, 0)),
                pl.BlockSpec((1, width), lambda i, c: (0, 0)),
                pl.BlockSpec(memory_space=pl.ANY),
            ],
            out_specs=places,
        ),
        out_shape=shapes,
        input_output_aliases={} if base is None else {3: 0},
        name="half_rows",
    )(choice, states, gain, *held)


def columns_kernel(x, vision, out):
    copies, z, _, width = out.shape
    span = width // x
    for c in range(copies):
        for k in range(z):
            for j in range(x):
                start = (j * z + k) * span
                out[c, k, :, j * span : (j + 1) * span] = vision[:, start : start + span]


def columns_of(vision, copies, x, z):
    tokens, width = vision.shape
    shape = (copies, z, tokens, width // z)
    return pl.pallas_call(
        functools.partial(columns_kernel, x),
        in_specs=[whole(vision.shape)],
        out_specs=whole(shape),
        grid=(1,),
        out_shape=jax.ShapeDtypeStruct(shape, vision.dtype),
        name="columns",
    )(vision)


def partial_kernel(spot, here, there, *rest):
    *weights, out = rest
    z, _, yl, tokens, width = out.shape
    x = len(weights)
    span = weights[0].shape[0]
    for c, part in enumerate((here, there)):
        product = jnp.zeros((part.shape[0], width), jnp.float32)
        for k, weight in enumerate(weights):
            start = pl.multiple_of(lax.rem(spot[0] + x - k, x) * span, span)
            product += jnp.dot(
                part[:, pl.ds(start, span)], weight[...], preferred_element_type=jnp.float32
            )
        for a in range(yl):
            for k in range(z):
                row = (a * z + k) * tokens
                out[k, c, a] = product[row : row + tokens]


def partial_sums(here, there, spot, weights, z, yl, tokens):
    shape = (z, 2, yl, tokens, weights[0].shape[1])
    return pl.pallas_call(
        partial_kernel,
        in_specs=[scalar, whole(here.shape), whole(there.shape), *(whole(w.shape) for w in weights)],
        out_specs=whole(shape),
        grid=(1,),
        out_shape=jax.ShapeDtypeStruct(shape, jnp.float32),
        name="partial_sums",
    )(spot, here, there, *weights)


def pair_kernel(odd, parts, k_gain, out):
    sources, cores, yl, tokens, width = parts.shape
    head = width // 2
    copies = out.shape[0]
    swap = odd[0] != 0
    total = parts[0]
    for s in range(1, sources):
        total = total + parts[s]
    rows = jnp.concatenate([total[c, a] for c in range(cores) for a in range(yl)], axis=0)
    keys = head_norm(rows[:, :head], k_gain[...]).astype(out.dtype)
    values = rows[:, head:].astype(out.dtype)
    half = yl * tokens
    for a in range(yl):
        near = slice(a * tokens, (a + 1) * tokens)
        far = slice(half + a * tokens, half + (a + 1) * tokens)
        for piece, lanes in ((keys, slice(0, head)), (values, slice(head, width))):
            even_core = jnp.where(swap, piece[far], piece[near])
            odd_core = jnp.where(swap, piece[near], piece[far])
            for c in range(copies):
                out[c, 2 * a, :, lanes] = even_core
                out[c, 2 * a + 1, :, lanes] = odd_core


def pairs_of(odd, parts, k_gain, copies):
    _, cores, yl, tokens, width = parts.shape
    shape = (copies, cores * yl, tokens, width)
    return pl.pallas_call(
        pair_kernel,
        in_specs=[scalar, whole(parts.shape), whole(k_gain.shape)],
        out_specs=whole(shape),
        grid=(1,),
        out_shape=jax.ShapeDtypeStruct(shape, jnp.bfloat16),
        name="key_value_pairs",
    )(odd, parts, k_gain)


def attention_kernel(
    core, owners, counts, gate, query, near, far, q_gain, own, after, before, low, high, out
):
    block = pl.program_id(0)
    rows, width = query.shape
    images = own.shape[0]
    half = low.shape[0]
    head = q_gain.shape[1]
    heads = width // head
    slots = owners.shape[1]
    scale = head ** (-0.5)
    gain = q_gain[...]
    span = near.shape[0]
    first = block * rows
    inside = lax.rem(first, span)
    at = pl.ds(pl.multiple_of(inside, rows), rows)
    total = query[...] + jnp.where(first // span == core[0], near[at, :], far[at, :])
    parts = []
    for h in range(heads):
        parts.append(head_norm(total[:, h * head : (h + 1) * head], gain).astype(jnp.bfloat16))
    queries = jnp.concatenate(parts, axis=0)
    count = counts[block]
    names = [owners[block, j] for j in range(slots)]
    scores = []
    values = []
    live = jnp.bool_(False)
    for j in range(slots):
        valid = j < count
        for i in range(j):
            valid = valid & (names[i] != names[j])
        live = live | valid
        image = jnp.clip(names[j], 0, images - 1)
        lower = jnp.minimum(image, half - 1)
        upper = jnp.maximum(image - half, 0)
        across = jnp.where(image < half, low[lower], high[upper])
        pairs = jnp.concatenate((own[image], after[image], before[image], across), axis=0)
        values.append(pairs[:, head:])
        score = (
            lax.dot_general(
                queries, pairs[:, :head], (((1,), (1,)), ((), ())), preferred_element_type=jnp.float32
            )
            * scale
        )
        scores.append(jnp.where(valid, score, masked_score))
    top = jnp.max(scores[0], axis=1, keepdims=True)
    for j in range(1, slots):
        top = jnp.maximum(top, jnp.max(scores[j], axis=1, keepdims=True))
    denominator = jnp.zeros_like(top)
    numerator = jnp.zeros((rows * heads, head), jnp.float32)
    for j in range(slots):
        weights = jnp.exp(scores[j] - top).astype(jnp.bfloat16)
        denominator += jnp.sum(weights.astype(jnp.float32), axis=1, keepdims=True)
        numerator += jnp.dot(weights, values[j], preferred_element_type=jnp.float32)
    factor = jnp.where(live, gate[0], 0.0)
    attended = (numerator / denominator * factor).astype(out.dtype)
    for h in range(heads):
        out[:, h * head : (h + 1) * head] = attended[h * rows : (h + 1) * rows]


def attention(core, owners, counts, gate_value, query, near, far, q_gain, pieces):
    blocks = owners.shape[0]
    tokens, width = query.shape
    rows = tokens // blocks
    return pl.pallas_call(
        attention_kernel,
        grid=(blocks,),
        in_specs=[
            *(scalar,) * 4,
            pl.BlockSpec((rows, width), lambda b: (b, 0)),
            whole(near.shape),
            whole(far.shape),
            whole(q_gain.shape),
            *(whole(p.shape) for p in pieces),
        ],
        out_specs=pl.BlockSpec((rows, width), lambda b: (b, 0)),
        out_shape=jax.ShapeDtypeStruct((tokens, width), jnp.bfloat16),
        name="attention",
    )(core, owners, counts, gate_value, query, near, far, q_gain, *pieces)


def on_device(
    text_states,
    text_gain,
    vision,
    q_weight,
    k_weight,
    v_weight,
    q_gain,
    k_gain,
    owners,
    counts,
    gate_value,
):
    head = q_gain.shape[0]
    tokens = vision.shape[1]
    width = text_states.shape[1]
    yl, co, x, z, yh = (lax.axis_size(a) for a in IMG + FSDP)
    first = lax.axis_index("yh") == 0

    q_half = lax.all_gather(q_weight, ("x", "z"), axis=0, tiled=True)

    columns = columns_of(vision.reshape(tokens, width), yl, x, z)
    here = exchange(columns.reshape(yl * z, tokens, width // z), ("yl", "z"))

    joined = jnp.concatenate((k_weight, v_weight), axis=1)
    other = shift(joined, "yh", 1)
    both = jnp.where(
        first,
        jnp.concatenate((joined, other), axis=0),
        jnp.concatenate((other, joined), axis=0),
    )
    pair_weight = (both, *(shift(both, "x", k) for k in range(1, x)))

    gate = jnp.tanh(gate_value)

    core = lax.axis_index("co")
    mine = lax.axis_index("yh")
    gain = text_gain[None]
    choice = jnp.stack((core, mine)).astype(jnp.int32)
    text_half, sent = half_rows(text_states, gain, choice, None)
    guest = shift(sent, "yh", 1)
    guest_other = shift(guest, "co", 1)
    choice = jnp.stack((1 - core, mine)).astype(jnp.int32)
    (text_half,) = half_rows(text_states, gain, choice, text_half)

    there = shift(here, "co", 1)
    partial = partial_sums(
        here.reshape(yl * z * tokens, width // z),
        there.reshape(yl * z * tokens, width // z),
        lax.axis_index("x").astype(jnp.int32)[None],
        pair_weight,
        z,
        yl,
        tokens,
    )
    parts = exchange(partial, "z")
    odd = lax.axis_index("co").astype(jnp.int32)[None]
    pair = pairs_of(odd, parts, k_gain[None], z * yh)
    own = exchange(pair, ("z", "yh"))
    own = own.transpose(1, 0, 2, 3).reshape(yl * co, z * yh * tokens, 2 * head)
    after = shift(own, "x", 1)
    before = shift(own, "x", -1)
    half = yl * co // 2
    low = shift(after[:half], "x", 1)
    high = shift(before[half:], "x", -1)

    guest_near = jnp.dot(guest, q_half, preferred_element_type=jnp.float32)
    guest_far = jnp.dot(guest_other, q_half, preferred_element_type=jnp.float32)
    back_near = shift(guest_near, "yh", 1)
    back_far = shift(guest_far, "yh", 1)
    query = jnp.dot(text_half, q_half, preferred_element_type=jnp.float32)
    return attention(
        core.astype(jnp.int32)[None],
        owners,
        counts,
        gate,
        query,
        back_near,
        back_far,
        q_gain[None],
        (own, after, before, low, high),
    )


def solution(mesh):
    fine = Mesh(mesh.devices.reshape(SIZES), IMG + FSDP)
    in_specs = (
        P(FSDP, None),
        P(),
        P(IMG, FSDP, None),
        P(FSDP, IMG),
        P(FSDP, IMG),
        P(FSDP, IMG),
        P(),
        P(),
        P(FSDP, None),
        P(FSDP),
        P(),
    )
    return jax.shard_map(
        on_device, mesh=fine, in_specs=in_specs, out_specs=P(FSDP, IMG), check_vma=False
    )
```

```python
import functools

import jax
import jax.numpy as jnp
from jax import lax
from jax.experimental import pallas as pl
from jax.experimental.pallas import tpu as pltpu
from jax.sharding import Mesh, PartitionSpec as P


norm_epsilon = 1e-05
masked_score = -1e30


IMG = ("yl", "co")
FSDP = ("x", "z", "yh")
SIZES = (4, 2, 4, 8, 2)


def shift(array, axis, step):
    size = lax.axis_size(axis)
    return lax.ppermute(array, axis, [(i, (i + step) % size) for i in range(size)])


def exchange(array, axes):
    return lax.all_to_all(array, axes, 0, 0, tiled=True)


def head_norm(values, gain):
    mean_square = jnp.mean(values * values, axis=-1, keepdims=True)
    return values * lax.rsqrt(mean_square + norm_epsilon) * gain


def whole(shape):
    return pl.BlockSpec(shape, lambda *_: (0,) * len(shape))


scalar = pl.BlockSpec(memory_space=pltpu.SMEM)


def half_kernel(x, z, choice, states, gain, *rest):
    outs = rest[1:]
    rows, width = states.shape
    depth = 128
    span = width // (x * z)
    squares = jnp.zeros((rows, depth), jnp.float32)
    for j in range(width // depth):
        wide = states[:, j * depth : (j + 1) * depth].astype(jnp.float32)
        squares += wide * wide
    scale = lax.rsqrt(jnp.sum(squares, axis=-1, keepdims=True) / width + norm_epsilon)
    even = choice[1] == 0
    for k in range(z):
        for m in range(x // 2):
            blocks = []
            for p in range(2):
                start = ((2 * m + p) * z + k) * span
                at = slice(start, start + span)
                wide = states[:, at].astype(jnp.float32)
                blocks.append((wide * scale * gain[:, at]).astype(jnp.bfloat16))
            start = (k * (x // 2) + m) * span
            lanes = slice(start, start + span)
            outs[0][:, lanes] = jnp.where(even, blocks[0], blocks[1])
            if len(outs) > 1:
                outs[1][:, lanes] = jnp.where(even, blocks[1], blocks[0])


def half_rows(states, gain, choice, base, x, z):
    total, width = states.shape
    rows = 32
    steps = total // 2 // rows
    held = () if base is None else (base,)
    place = pl.BlockSpec((rows, width // 2), lambda i, c: (c[0] * steps + i, 0))
    shapes = [jax.ShapeDtypeStruct((total, width // 2), jnp.bfloat16)]
    places = [place]
    if base is None:
        held = (gain,)
        shapes.append(jax.ShapeDtypeStruct((total // 2, width // 2), jnp.bfloat16))
        places.append(pl.BlockSpec((rows, width // 2), lambda i, c: (i, 0)))
    return pl.pallas_call(
        functools.partial(half_kernel, x, z),
        grid_spec=pltpu.PrefetchScalarGridSpec(
            num_scalar_prefetch=1,
            grid=(steps,),
            in_specs=[
                pl.BlockSpec((rows, width), lambda i, c: (c[0] * steps + i, 0)),
                pl.BlockSpec((1, width), lambda i, c: (0, 0)),
                pl.BlockSpec(memory_space=pl.ANY),
            ],
            out_specs=places,
        ),
        out_shape=shapes,
        input_output_aliases={} if base is None else {3: 0},
        name="half_rows",
    )(choice, states, gain, *held)


def join_kernel(*refs):
    *parts, out = refs
    start = 0
    for part in parts:
        width = part.shape[1]
        out[:, start : start + width] = part[...]
        start += width


def join(*parts):
    shape = (parts[0].shape[0], sum(p.shape[1] for p in parts))
    return pl.pallas_call(
        join_kernel,
        in_specs=[whole(p.shape) for p in parts],
        out_specs=whole(shape),
        grid=(1,),
        out_shape=jax.ShapeDtypeStruct(shape, parts[0].dtype),
        name="join",
    )(*parts)


def columns_kernel(x, vision, out):
    copies, z, _, width = out.shape
    span = width // x
    for c in range(copies):
        for k in range(z):
            for j in range(x):
                start = (j * z + k) * span
                out[c, k, :, j * span : (j + 1) * span] = vision[:, start : start + span]


def columns_of(vision, copies, x, z):
    tokens, width = vision.shape
    shape = (copies, z, tokens, width // z)
    return pl.pallas_call(
        functools.partial(columns_kernel, x),
        in_specs=[whole(vision.shape)],
        out_specs=whole(shape),
        grid=(1,),
        out_shape=jax.ShapeDtypeStruct(shape, vision.dtype),
        name="columns",
    )(vision)


def partial_kernel(spot, here, there, *rest):
    *weights, out = rest
    z, _, yl, tokens, width = out.shape
    x = len(weights)
    span = weights[0].shape[0]
    for c, part in enumerate((here, there)):
        product = jnp.zeros((part.shape[0], width), jnp.float32)
        for k, weight in enumerate(weights):
            start = pl.multiple_of(lax.rem(spot[0] + x - k, x) * span, span)
            product += jnp.dot(
                part[:, pl.ds(start, span)], weight[...], preferred_element_type=jnp.float32
            )
        for a in range(yl):
            for k in range(z):
                row = (a * z + k) * tokens
                out[k, c, a] = product[row : row + tokens]


def partial_sums(here, there, spot, weights, width, z, yl, tokens):
    shape = (z, 2, yl, tokens, width)
    return pl.pallas_call(
        partial_kernel,
        in_specs=[
            scalar,
            whole(here.shape),
            whole(there.shape),
            *(whole((w.shape[0], width)) for w in weights),
        ],
        out_specs=whole(shape),
        grid=(1,),
        out_shape=jax.ShapeDtypeStruct(shape, jnp.float32),
        name="partial_sums",
    )(spot, here, there, *weights)


def pair_kernel(odd, parts, k_gain, out):
    sources, cores, yl, tokens, width = parts.shape
    head = width // 2
    copies = out.shape[0]
    swap = odd[0] != 0
    total = parts[0]
    for s in range(1, sources):
        total = total + parts[s]
    rows = jnp.concatenate([total[c, a] for c in range(cores) for a in range(yl)], axis=0)
    keys = head_norm(rows[:, :head], k_gain[...]).astype(out.dtype)
    values = rows[:, head:].astype(out.dtype)
    half = yl * tokens
    for a in range(yl):
        near = slice(a * tokens, (a + 1) * tokens)
        far = slice(half + a * tokens, half + (a + 1) * tokens)
        for piece, lanes in ((keys, slice(0, head)), (values, slice(head, width))):
            even_core = jnp.where(swap, piece[far], piece[near])
            odd_core = jnp.where(swap, piece[near], piece[far])
            for c in range(copies):
                out[c, 2 * a, :, lanes] = even_core
                out[c, 2 * a + 1, :, lanes] = odd_core


def pairs_of(odd, parts, k_gain, copies):
    _, cores, yl, tokens, width = parts.shape
    shape = (copies, cores * yl, tokens, width)
    return pl.pallas_call(
        pair_kernel,
        in_specs=[scalar, whole(parts.shape), whole(k_gain.shape)],
        out_specs=whole(shape),
        grid=(1,),
        out_shape=jax.ShapeDtypeStruct(shape, jnp.bfloat16),
        name="key_value_pairs",
    )(odd, parts, k_gain)


def attention_kernel(
    core, owners, counts, gate, query, near, far, q_gain, own, after, before, low, high, out
):
    block = pl.program_id(0)
    rows, width = query.shape
    images = own.shape[0]
    half = low.shape[0]
    head = q_gain.shape[1]
    heads = width // head
    slots = owners.shape[1]
    scale = head ** (-0.5)
    gain = q_gain[...]
    span = near.shape[0]
    first = block * rows
    inside = lax.rem(first, span)
    at = pl.ds(pl.multiple_of(inside, rows), rows)
    total = query[...] + jnp.where(first // span == core[0], near[at, :], far[at, :])
    parts = []
    for h in range(heads):
        parts.append(head_norm(total[:, h * head : (h + 1) * head], gain).astype(jnp.bfloat16))
    queries = jnp.concatenate(parts, axis=0)
    count = counts[block]
    names = [owners[block, j] for j in range(slots)]
    scores = []
    values = []
    live = jnp.bool_(False)
    for j in range(slots):
        valid = j < count
        for i in range(j):
            valid = valid & (names[i] != names[j])
        live = live | valid
        image = jnp.clip(names[j], 0, images - 1)
        lower = jnp.minimum(image, half - 1)
        upper = jnp.maximum(image - half, 0)
        across = jnp.where(image < half, low[lower], high[upper])
        pairs = jnp.concatenate((own[image], after[image], before[image], across), axis=0)
        values.append(pairs[:, head:])
        score = (
            lax.dot_general(
                queries, pairs[:, :head], (((1,), (1,)), ((), ())), preferred_element_type=jnp.float32
            )
            * scale
        )
        scores.append(jnp.where(valid, score, masked_score))
    top = jnp.max(scores[0], axis=1, keepdims=True)
    for j in range(1, slots):
        top = jnp.maximum(top, jnp.max(scores[j], axis=1, keepdims=True))
    denominator = jnp.zeros_like(top)
    numerator = jnp.zeros((rows * heads, head), jnp.float32)
    for j in range(slots):
        weights = jnp.exp(scores[j] - top).astype(jnp.bfloat16)
        denominator += jnp.sum(weights.astype(jnp.float32), axis=1, keepdims=True)
        numerator += jnp.dot(weights, values[j], preferred_element_type=jnp.float32)
    factor = jnp.where(live, gate[0], 0.0)
    attended = (numerator / denominator * factor).astype(out.dtype)
    for h in range(heads):
        out[:, h * head : (h + 1) * head] = attended[h * rows : (h + 1) * rows]


def attention(core, owners, counts, gate_value, query, near, far, q_gain, pieces):
    blocks = owners.shape[0]
    tokens, width = query.shape
    rows = tokens // blocks
    return pl.pallas_call(
        attention_kernel,
        grid=(blocks,),
        in_specs=[
            *(scalar,) * 4,
            pl.BlockSpec((rows, width), lambda b: (b, 0)),
            whole(near.shape),
            whole(far.shape),
            whole(q_gain.shape),
            *(whole(p.shape) for p in pieces),
        ],
        out_specs=pl.BlockSpec((rows, width), lambda b: (b, 0)),
        out_shape=jax.ShapeDtypeStruct((tokens, width), jnp.bfloat16),
        name="attention",
    )(core, owners, counts, gate_value, query, near, far, q_gain, *pieces)


def on_device(
    text_states,
    text_gain,
    vision,
    q_weight,
    k_weight,
    v_weight,
    q_gain,
    k_gain,
    owners,
    counts,
    gate_value,
):
    head = q_gain.shape[0]
    tokens = vision.shape[1]
    width = text_states.shape[1]
    yl, co, x, z, yh = (lax.axis_size(a) for a in IMG + FSDP)
    place = lax.axis_index("x")
    core = lax.axis_index("co")

    def ordered(early, mine, other):
        return jnp.where(
            early,
            jnp.concatenate((mine, other), axis=0),
            jnp.concatenate((other, mine), axis=0),
        )

    joined = join(k_weight, v_weight, q_weight)
    other = shift(joined, "yh", 1)
    both = ordered(lax.axis_index("yh") == 0, joined, other)
    far = shift(both, "x", 2)
    near = both[:, : 2 * head]
    pair_weight = (both, shift(near, "x", 1), far, shift(near, "x", 3))

    rows_q = ordered(place < 2, both[:, 2 * head :], far[:, 2 * head :])
    q_half = lax.all_gather(rows_q, "z", axis=0, tiled=True)

    columns = columns_of(vision.reshape(tokens, width), yl, x, z)
    here = exchange(columns.reshape(yl * z, tokens, width // z), ("yl", "z"))

    gate = jnp.tanh(gate_value)

    mine = lax.rem(place, 2)
    gain = text_gain[None]

    def partner(array):
        return lax.ppermute(array, "x", [(i, i ^ 1) for i in range(x)])

    choice = jnp.stack((core, mine)).astype(jnp.int32)
    text_half, sent = half_rows(text_states, gain, choice, None, x, z)
    guest = partner(sent)
    guest_other = shift(guest, "co", 1)
    choice = jnp.stack((1 - core, mine)).astype(jnp.int32)
    (text_half,) = half_rows(text_states, gain, choice, text_half, x, z)

    there = shift(here, "co", 1)
    partial = partial_sums(
        here.reshape(yl * z * tokens, width // z),
        there.reshape(yl * z * tokens, width // z),
        place.astype(jnp.int32)[None],
        pair_weight,
        2 * head,
        z,
        yl,
        tokens,
    )
    parts = exchange(partial, "z")
    odd = lax.axis_index("co").astype(jnp.int32)[None]
    pair = pairs_of(odd, parts, k_gain[None], z * yh)
    own = exchange(pair, ("z", "yh"))
    own = own.transpose(1, 0, 2, 3).reshape(yl * co, z * yh * tokens, 2 * head)
    after = shift(own, "x", 1)
    before = shift(own, "x", -1)
    half = yl * co // 2
    low = shift(after[:half], "x", 1)
    high = shift(before[half:], "x", -1)

    guest_near = jnp.dot(guest, q_half, preferred_element_type=jnp.float32)
    guest_far = jnp.dot(guest_other, q_half, preferred_element_type=jnp.float32)
    back_near = partner(guest_near)
    back_far = partner(guest_far)
    query = jnp.dot(text_half, q_half, preferred_element_type=jnp.float32)
    return attention(
        core.astype(jnp.int32)[None],
        owners,
        counts,
        gate,
        query,
        back_near,
        back_far,
        q_gain[None],
        (own, after, before, low, high),
    )


def solution(mesh):
    fine = Mesh(mesh.devices.reshape(SIZES), IMG + FSDP)
    in_specs = (
        P(FSDP, None),
        P(),
        P(IMG, FSDP, None),
        P(FSDP, IMG),
        P(FSDP, IMG),
        P(FSDP, IMG),
        P(),
        P(),
        P(FSDP, None),
        P(FSDP),
        P(),
    )
    return jax.shard_map(
        on_device, mesh=fine, in_specs=in_specs, out_specs=P(FSDP, IMG), check_vma=False
    )
```

```python
import functools

import jax
import jax.numpy as jnp
from jax import lax
from jax.experimental import pallas as pl
from jax.experimental.pallas import tpu as pltpu
from jax.sharding import Mesh, PartitionSpec as P


norm_epsilon = 1e-05
masked_score = -1e30


IMG = ("yl", "co")
FSDP = ("x", "z", "yh")
SIZES = (4, 2, 4, 8, 2)


def shift(array, axis, step):
    size = lax.axis_size(axis)
    return lax.ppermute(array, axis, [(i, (i + step) % size) for i in range(size)])


def exchange(array, axes):
    return lax.all_to_all(array, axes, 0, 0, tiled=True)


def head_norm(values, gain):
    mean_square = jnp.mean(values * values, axis=-1, keepdims=True)
    return values * lax.rsqrt(mean_square + norm_epsilon) * gain


def whole(shape):
    return pl.BlockSpec(shape, lambda *_: (0,) * len(shape))


scalar = pl.BlockSpec(memory_space=pltpu.SMEM)


def text_kernel(x, choice, states, gain, *rest):
    outs = rest[1:]
    rows, width = states.shape
    depth = 128
    squares = jnp.zeros((rows, depth), jnp.float32)
    for j in range(width // depth):
        wide = states[:, j * depth : (j + 1) * depth].astype(jnp.float32)
        squares += wide * wide
    scale = lax.rsqrt(jnp.sum(squares, axis=-1, keepdims=True) / width + norm_epsilon)
    span = width // x
    step = 2 * depth
    for k in range(x if len(outs) > 1 else 1):
        first = lax.rem(choice[1] + k, x) * span
        for j in range(span // step):
            at = pl.ds(pl.multiple_of(first + j * step, step), step)
            block = (states[:, at].astype(jnp.float32) * scale * gain[:, at]).astype(jnp.bfloat16)
            lanes = slice(j * step, (j + 1) * step)
            if k == 0:
                outs[0][:, lanes] = block
            else:
                outs[k][:, lanes] = block


def text_rows(states, gain, choice, base, x):
    total, width = states.shape
    rows = 32
    steps = total // 2 // rows
    span = width // x
    place = pl.BlockSpec((rows, span), lambda i, c: (c[0] * steps + i, 0))
    shapes = [jax.ShapeDtypeStruct((total, span), jnp.bfloat16)]
    places = [place]
    if base is None:
        shapes += [jax.ShapeDtypeStruct((total // 2, span), jnp.bfloat16)] * (x - 1)
        places += [pl.BlockSpec((rows, span), lambda i, c: (i, 0))] * (x - 1)
    return pl.pallas_call(
        functools.partial(text_kernel, x),
        grid_spec=pltpu.PrefetchScalarGridSpec(
            num_scalar_prefetch=1,
            grid=(steps,),
            in_specs=[
                pl.BlockSpec((rows, width), lambda i, c: (c[0] * steps + i, 0)),
                pl.BlockSpec((1, width), lambda i, c: (0, 0)),
                pl.BlockSpec(memory_space=pl.ANY),
            ],
            out_specs=places,
        ),
        out_shape=shapes,
        input_output_aliases={} if base is None else {3: 0},
        name="text_rows",
    )(choice, states, gain, gain if base is None else base)


def query_kernel(near, far, own, weight, query, *backs):
    rows = near.shape[0] // len(backs)
    columns = weight[...]
    for c, guests in enumerate((near, far)):
        product = jnp.dot(guests[...], columns, preferred_element_type=jnp.float32)
        for k, back in enumerate(backs):
            back[c * rows : (c + 1) * rows] = product[k * rows : (k + 1) * rows]
    query[...] = jnp.dot(own[...], columns, preferred_element_type=jnp.float32)


def query_products(near, far, own, weight, guests):
    rows = own.shape[0]
    depth, width = weight.shape
    block = width // 2
    column = pl.BlockSpec((rows, block), lambda n: (0, n))
    return pl.pallas_call(
        query_kernel,
        grid=(2,),
        in_specs=[
            whole(near.shape),
            whole(far.shape),
            whole(own.shape),
            pl.BlockSpec((depth, block), lambda n: (0, n)),
        ],
        out_specs=[column] * (1 + guests),
        out_shape=[jax.ShapeDtypeStruct((rows, width), jnp.float32)] * (1 + guests),
        name="query_products",
    )(near, far, own, weight)


def join_kernel(*refs):
    *parts, out = refs
    start = 0
    for part in parts:
        width = part.shape[1]
        out[:, start : start + width] = part[...]
        start += width


def join(*parts):
    shape = (parts[0].shape[0], sum(p.shape[1] for p in parts))
    return pl.pallas_call(
        join_kernel,
        in_specs=[whole(p.shape) for p in parts],
        out_specs=whole(shape),
        grid=(1,),
        out_shape=jax.ShapeDtypeStruct(shape, parts[0].dtype),
        name="join",
    )(*parts)


def columns_kernel(x, vision, out):
    copies, z, _, width = out.shape
    span = width // x
    for c in range(copies):
        for k in range(z):
            for j in range(x):
                start = (j * z + k) * span
                out[c, k, :, j * span : (j + 1) * span] = vision[:, start : start + span]


def columns_of(vision, copies, x, z):
    tokens, width = vision.shape
    shape = (copies, z, tokens, width // z)
    return pl.pallas_call(
        functools.partial(columns_kernel, x),
        in_specs=[whole(vision.shape)],
        out_specs=whole(shape),
        grid=(1,),
        out_shape=jax.ShapeDtypeStruct(shape, vision.dtype),
        name="columns",
    )(vision)


def partial_kernel(spot, here, there, *rest):
    *weights, out = rest
    z, _, yl, tokens, width = out.shape
    x = len(weights)
    span = weights[0].shape[0]
    for c, part in enumerate((here, there)):
        product = jnp.zeros((part.shape[0], width), jnp.float32)
        for k, weight in enumerate(weights):
            start = pl.multiple_of(lax.rem(spot[0] + x - k, x) * span, span)
            product += jnp.dot(
                part[:, pl.ds(start, span)], weight[...], preferred_element_type=jnp.float32
            )
        for a in range(yl):
            for k in range(z):
                row = (a * z + k) * tokens
                out[k, c, a] = product[row : row + tokens]


def partial_sums(here, there, spot, weights, width, z, yl, tokens):
    shape = (z, 2, yl, tokens, width)
    return pl.pallas_call(
        partial_kernel,
        in_specs=[
            scalar,
            whole(here.shape),
            whole(there.shape),
            *(whole((w.shape[0], width)) for w in weights),
        ],
        out_specs=whole(shape),
        grid=(1,),
        out_shape=jax.ShapeDtypeStruct(shape, jnp.float32),
        name="partial_sums",
    )(spot, here, there, *weights)


def pair_kernel(odd, parts, k_gain, out):
    sources, cores, yl, tokens, width = parts.shape
    head = width // 2
    copies = out.shape[0]
    swap = odd[0] != 0
    total = parts[0]
    for s in range(1, sources):
        total = total + parts[s]
    rows = jnp.concatenate([total[c, a] for c in range(cores) for a in range(yl)], axis=0)
    keys = head_norm(rows[:, :head], k_gain[...]).astype(out.dtype)
    values = rows[:, head:].astype(out.dtype)
    half = yl * tokens
    for a in range(yl):
        near = slice(a * tokens, (a + 1) * tokens)
        far = slice(half + a * tokens, half + (a + 1) * tokens)
        for piece, lanes in ((keys, slice(0, head)), (values, slice(head, width))):
            even_core = jnp.where(swap, piece[far], piece[near])
            odd_core = jnp.where(swap, piece[near], piece[far])
            for c in range(copies):
                out[c, 2 * a, :, lanes] = even_core
                out[c, 2 * a + 1, :, lanes] = odd_core


def pairs_of(odd, parts, k_gain, copies):
    _, cores, yl, tokens, width = parts.shape
    shape = (copies, cores * yl, tokens, width)
    return pl.pallas_call(
        pair_kernel,
        in_specs=[scalar, whole(parts.shape), whole(k_gain.shape)],
        out_specs=whole(shape),
        grid=(1,),
        out_shape=jax.ShapeDtypeStruct(shape, jnp.bfloat16),
        name="key_value_pairs",
    )(odd, parts, k_gain)


def attention_kernel(
    core, owners, counts, gate, query, share_1, share_2, share_3, q_gain, own, after, before, low, high, out
):
    block = pl.program_id(0)
    rows, width = query.shape
    images = own.shape[0]
    half = low.shape[0]
    head = q_gain.shape[1]
    heads = width // head
    slots = owners.shape[1]
    scale = head ** (-0.5)
    gain = q_gain[...]
    span = share_1.shape[0] // 2
    first = block * rows
    start = jnp.where(first // span == core[0], 0, span) + lax.rem(first, span)
    at = pl.ds(pl.multiple_of(start, rows), rows)
    total = query[...] + share_1[at, :] + share_2[at, :] + share_3[at, :]
    parts = []
    for h in range(heads):
        parts.append(head_norm(total[:, h * head : (h + 1) * head], gain).astype(jnp.bfloat16))
    queries = jnp.concatenate(parts, axis=0)
    count = counts[block]
    names = [owners[block, j] for j in range(slots)]
    scores = []
    values = []
    live = jnp.bool_(False)
    for j in range(slots):
        valid = j < count
        for i in range(j):
            valid = valid & (names[i] != names[j])
        live = live | valid
        image = jnp.clip(names[j], 0, images - 1)
        lower = jnp.minimum(image, half - 1)
        upper = jnp.maximum(image - half, 0)
        across = jnp.where(image < half, low[lower], high[upper])
        pairs = jnp.concatenate((own[image], after[image], before[image], across), axis=0)
        values.append(pairs[:, head:])
        score = (
            lax.dot_general(
                queries, pairs[:, :head], (((1,), (1,)), ((), ())), preferred_element_type=jnp.float32
            )
            * scale
        )
        scores.append(jnp.where(valid, score, masked_score))
    top = jnp.max(scores[0], axis=1, keepdims=True)
    for j in range(1, slots):
        top = jnp.maximum(top, jnp.max(scores[j], axis=1, keepdims=True))
    denominator = jnp.zeros_like(top)
    numerator = jnp.zeros((rows * heads, head), jnp.float32)
    for j in range(slots):
        weights = jnp.exp(scores[j] - top).astype(jnp.bfloat16)
        denominator += jnp.sum(weights.astype(jnp.float32), axis=1, keepdims=True)
        numerator += jnp.dot(weights, values[j], preferred_element_type=jnp.float32)
    factor = jnp.where(live, gate[0], 0.0)
    attended = (numerator / denominator * factor).astype(out.dtype)
    for h in range(heads):
        out[:, h * head : (h + 1) * head] = attended[h * rows : (h + 1) * rows]


def attention(core, owners, counts, gate_value, query, shares, q_gain, pieces):
    blocks = owners.shape[0]
    tokens, width = query.shape
    rows = tokens // blocks
    return pl.pallas_call(
        attention_kernel,
        grid=(blocks,),
        in_specs=[
            *(scalar,) * 4,
            pl.BlockSpec((rows, width), lambda b: (b, 0)),
            *(whole(share.shape) for share in shares),
            whole(q_gain.shape),
            *(whole(p.shape) for p in pieces),
        ],
        out_specs=pl.BlockSpec((rows, width), lambda b: (b, 0)),
        out_shape=jax.ShapeDtypeStruct((tokens, width), jnp.bfloat16),
        name="attention",
    )(core, owners, counts, gate_value, query, *shares, q_gain, *pieces)


def on_device(
    text_states,
    text_gain,
    vision,
    q_weight,
    k_weight,
    v_weight,
    q_gain,
    k_gain,
    owners,
    counts,
    gate_value,
):
    head = q_gain.shape[0]
    tokens = vision.shape[1]
    width = text_states.shape[1]
    yl, co, x, z, yh = (lax.axis_size(a) for a in IMG + FSDP)
    place = lax.axis_index("x")
    core = lax.axis_index("co")

    def ordered(early, mine, other):
        return jnp.where(
            early,
            jnp.concatenate((mine, other), axis=0),
            jnp.concatenate((other, mine), axis=0),
        )

    joined = join(k_weight, v_weight, q_weight)
    other = shift(joined, "yh", 1)
    both = ordered(lax.axis_index("yh") == 0, joined, other)
    near = both[:, : 2 * head]
    pair_weight = (near, *(shift(near, "x", k) for k in range(1, x)))

    q_part = lax.all_gather(both[:, 2 * head :], "z", axis=0, tiled=True)

    columns = columns_of(vision.reshape(tokens, width), yl, x, z)
    here = exchange(columns.reshape(yl * z, tokens, width // z), ("yl", "z"))

    gate = jnp.tanh(gate_value)

    gain = text_gain[None]
    choice = jnp.stack((core, place)).astype(jnp.int32)
    text_own, *sent = text_rows(text_states, gain, choice, None, x)
    came = [shift(part, "x", k + 1) for k, part in enumerate(sent)]
    guest = jnp.concatenate(came, axis=0)
    guest_other = shift(guest, "co", 1)
    choice = jnp.stack((1 - core, place)).astype(jnp.int32)
    (text_own,) = text_rows(text_states, gain, choice, text_own, x)

    there = shift(here, "co", 1)
    partial = partial_sums(
        here.reshape(yl * z * tokens, width // z),
        there.reshape(yl * z * tokens, width // z),
        place.astype(jnp.int32)[None],
        pair_weight,
        2 * head,
        z,
        yl,
        tokens,
    )
    parts = exchange(partial, "z")
    odd = lax.axis_index("co").astype(jnp.int32)[None]
    pair = pairs_of(odd, parts, k_gain[None], z * yh)
    own = exchange(pair, ("z", "yh"))
    own = own.transpose(1, 0, 2, 3).reshape(yl * co, z * yh * tokens, 2 * head)
    after = shift(own, "x", 1)
    before = shift(own, "x", -1)
    half = yl * co // 2
    low = shift(after[:half], "x", 1)
    high = shift(before[half:], "x", -1)

    query, *backs = query_products(guest, guest_other, text_own, q_part, x - 1)
    shares = [shift(part, "x", -(k + 1)) for k, part in enumerate(backs)]
    return attention(
        core.astype(jnp.int32)[None],
        owners,
        counts,
        gate,
        query,
        shares,
        q_gain[None],
        (own, after, before, low, high),
    )


def solution(mesh):
    fine = Mesh(mesh.devices.reshape(SIZES), IMG + FSDP)
    in_specs = (
        P(FSDP, None),
        P(),
        P(IMG, FSDP, None),
        P(FSDP, IMG),
        P(FSDP, IMG),
        P(FSDP, IMG),
        P(),
        P(),
        P(FSDP, None),
        P(FSDP),
        P(),
    )
    return jax.shard_map(
        on_device, mesh=fine, in_specs=in_specs, out_specs=P(FSDP, IMG), check_vma=False
    )
```

```python
import functools

import jax
import jax.numpy as jnp
from jax import lax
from jax.experimental import pallas as pl
from jax.experimental.pallas import tpu as pltpu
from jax.sharding import Mesh, PartitionSpec as P


norm_epsilon = 1e-05
masked_score = -1e30


IMG = ("yl", "co")
FSDP = ("x", "z", "yh")
SIZES = (4, 2, 4, 8, 2)


def shift(array, axis, step):
    size = lax.axis_size(axis)
    return lax.ppermute(array, axis, [(i, (i + step) % size) for i in range(size)])


def exchange(array, axes):
    return lax.all_to_all(array, axes, 0, 0, tiled=True)


def head_norm(values, gain):
    mean_square = jnp.mean(values * values, axis=-1, keepdims=True)
    return values * lax.rsqrt(mean_square + norm_epsilon) * gain


def whole(shape):
    return pl.BlockSpec(shape, lambda *_: (0,) * len(shape))


scalar = pl.BlockSpec(memory_space=pltpu.SMEM)


def half_kernel(x, z, yh, choice, states, gain, *rest):
    outs = rest[1:]
    rows, width = states.shape
    depth = width // (x * z * yh)
    squares = jnp.zeros((rows, depth), jnp.float32)
    for j in range(width // depth):
        wide = states[:, j * depth : (j + 1) * depth].astype(jnp.float32)
        squares += wide * wide
    scale = lax.rsqrt(jnp.sum(squares, axis=-1, keepdims=True) / width + norm_epsilon)
    for index, out in enumerate(outs):
        home = choice[1] if index == 0 else choice[1] + 1 - 2 * lax.rem(choice[1], 2)
        for k in range(z):
            for m in range(x // 2):
                for h in range(yh):
                    place = (lax.rem(home + 2 * m, x) * z + k) * yh + lax.rem(choice[2] + h, yh)
                    at = pl.ds(pl.multiple_of(place * depth, depth), depth)
                    wide = states[:, at].astype(jnp.float32)
                    start = ((k * (x // 2) + m) * yh + h) * depth
                    block = wide * scale * gain[:, at]
                    out[:, start : start + depth] = block.astype(out.dtype)


def half_rows(states, gain, choice, base, x, z, yh):
    total, width = states.shape
    rows = 32
    steps = total // 2 // rows
    held = () if base is None else (base,)
    place = pl.BlockSpec((rows, width // 2), lambda i, c: (c[0] * steps + i, 0))
    shapes = [jax.ShapeDtypeStruct((total, width // 2), jnp.bfloat16)]
    places = [place]
    if base is None:
        held = (gain,)
        shapes.append(jax.ShapeDtypeStruct((total // 2, width // 2), jnp.bfloat16))
        places.append(pl.BlockSpec((rows, width // 2), lambda i, c: (i, 0)))
    return pl.pallas_call(
        functools.partial(half_kernel, x, z, yh),
        grid_spec=pltpu.PrefetchScalarGridSpec(
            num_scalar_prefetch=1,
            grid=(steps,),
            in_specs=[
                pl.BlockSpec((rows, width), lambda i, c: (c[0] * steps + i, 0)),
                pl.BlockSpec((1, width), lambda i, c: (0, 0)),
                pl.BlockSpec(memory_space=pl.ANY),
            ],
            out_specs=places,
        ),
        out_shape=shapes,
        input_output_aliases={} if base is None else {3: 0},
        name="half_rows",
    )(choice, states, gain, *held)


def join_kernel(*refs):
    *parts, out = refs
    start = 0
    for part in parts:
        width = part.shape[1]
        out[:, start : start + width] = part[...]
        start += width


def join(*parts):
    shape = (parts[0].shape[0], sum(p.shape[1] for p in parts))
    return pl.pallas_call(
        join_kernel,
        in_specs=[whole(p.shape) for p in parts],
        out_specs=whole(shape),
        grid=(1,),
        out_shape=jax.ShapeDtypeStruct(shape, parts[0].dtype),
        name="join",
    )(*parts)


def pile_kernel(first, last, *refs):
    *parts, out = refs
    rows = parts[0].shape[0]
    for k, part in enumerate(parts):
        out[k * rows : (k + 1) * rows] = part[:, first:last]


def pile(parts, first, last):
    shape = (len(parts) * parts[0].shape[0], last - first)
    return pl.pallas_call(
        functools.partial(pile_kernel, first, last),
        in_specs=[whole(p.shape) for p in parts],
        out_specs=whole(shape),
        grid=(1,),
        out_shape=jax.ShapeDtypeStruct(shape, parts[0].dtype),
        name="pile",
    )(*parts)


def columns_kernel(x, vision, out):
    copies, z, _, width = out.shape
    span = width // x
    for c in range(copies):
        for k in range(z):
            for j in range(x):
                start = (j * z + k) * span
                out[c, k, :, j * span : (j + 1) * span] = vision[:, start : start + span]


def columns_of(vision, copies, x, z):
    tokens, width = vision.shape
    shape = (copies, z, tokens, width // z)
    return pl.pallas_call(
        functools.partial(columns_kernel, x),
        in_specs=[whole(vision.shape)],
        out_specs=whole(shape),
        grid=(1,),
        out_shape=jax.ShapeDtypeStruct(shape, vision.dtype),
        name="columns",
    )(vision)


def partial_kernel(x, spot, here, there, *rest):
    *weights, out = rest
    z, _, yl, tokens, _ = out.shape
    yh = len(weights) // x
    span = weights[0].shape[0]
    columns = jnp.concatenate([w[...] for w in weights], axis=0)
    starts = []
    for k in range(x):
        for h in range(yh):
            place = lax.rem(spot[0] + x - k, x) * yh + lax.rem(spot[1] + h, yh)
            starts.append(pl.multiple_of(place * span, span))
    for c, part in enumerate((here, there)):
        rows = jnp.concatenate([part[:, pl.ds(start, span)] for start in starts], axis=1)
        product = jnp.dot(rows, columns, preferred_element_type=jnp.float32)
        for a in range(yl):
            for k in range(z):
                row = (a * z + k) * tokens
                out[k, c, a] = product[row : row + tokens]


def partial_sums(here, there, spot, weights, width, x, z, yl, tokens):
    depth = here.shape[1] // len(weights)
    shape = (z, 2, yl, tokens, width)
    return pl.pallas_call(
        functools.partial(partial_kernel, x),
        in_specs=[
            scalar,
            whole(here.shape),
            whole(there.shape),
            *(pl.BlockSpec((depth, width), lambda _, r=r: (r, 0)) for _, r in weights),
        ],
        out_specs=whole(shape),
        grid=(1,),
        out_shape=jax.ShapeDtypeStruct(shape, jnp.float32),
        name="partial_sums",
    )(spot, here, there, *(w for w, _ in weights))


def pair_kernel(odd, parts, k_gain, out):
    sources, cores, yl, tokens, width = parts.shape
    head = width // 2
    copies = out.shape[0]
    swap = odd[0] != 0
    total = parts[0]
    for s in range(1, sources):
        total = total + parts[s]
    rows = jnp.concatenate([total[c, a] for c in range(cores) for a in range(yl)], axis=0)
    keys = head_norm(rows[:, :head], k_gain[...]).astype(out.dtype)
    values = rows[:, head:].astype(out.dtype)
    half = yl * tokens
    for a in range(yl):
        near = slice(a * tokens, (a + 1) * tokens)
        far = slice(half + a * tokens, half + (a + 1) * tokens)
        for piece, lanes in ((keys, slice(0, head)), (values, slice(head, width))):
            even_core = jnp.where(swap, piece[far], piece[near])
            odd_core = jnp.where(swap, piece[near], piece[far])
            for c in range(copies):
                out[c, 2 * a, :, lanes] = even_core
                out[c, 2 * a + 1, :, lanes] = odd_core


def pairs_of(odd, parts, k_gain, copies):
    _, cores, yl, tokens, width = parts.shape
    shape = (copies, cores * yl, tokens, width)
    return pl.pallas_call(
        pair_kernel,
        in_specs=[scalar, whole(parts.shape), whole(k_gain.shape)],
        out_specs=whole(shape),
        grid=(1,),
        out_shape=jax.ShapeDtypeStruct(shape, jnp.bfloat16),
        name="key_value_pairs",
    )(odd, parts, k_gain)


def attention_kernel(
    core, owners, counts, gate, query, near, far, q_gain, own, after, before, low, high, out
):
    block = pl.program_id(0)
    rows, width = query.shape
    images = own.shape[0]
    half = low.shape[0]
    head = q_gain.shape[1]
    heads = width // head
    slots = owners.shape[1]
    scale = head ** (-0.5)
    gain = q_gain[...]
    span = near.shape[0]
    first = block * rows
    inside = lax.rem(first, span)
    at = pl.ds(pl.multiple_of(inside, rows), rows)
    total = query[...] + jnp.where(first // span == core[0], near[at, :], far[at, :])
    parts = []
    for h in range(heads):
        parts.append(head_norm(total[:, h * head : (h + 1) * head], gain).astype(jnp.bfloat16))
    queries = jnp.concatenate(parts, axis=0)
    count = counts[block]
    names = [owners[block, j] for j in range(slots)]
    scores = []
    values = []
    live = jnp.bool_(False)
    for j in range(slots):
        valid = j < count
        for i in range(j):
            valid = valid & (names[i] != names[j])
        live = live | valid
        image = jnp.clip(names[j], 0, images - 1)
        lower = jnp.minimum(image, half - 1)
        upper = jnp.maximum(image - half, 0)
        across = jnp.where(image < half, low[lower], high[upper])
        pairs = jnp.concatenate((own[image], after[image], before[image], across), axis=0)
        values.append(pairs[:, head:])
        score = (
            lax.dot_general(
                queries, pairs[:, :head], (((1,), (1,)), ((), ())), preferred_element_type=jnp.float32
            )
            * scale
        )
        scores.append(jnp.where(valid, score, masked_score))
    top = jnp.max(scores[0], axis=1, keepdims=True)
    for j in range(1, slots):
        top = jnp.maximum(top, jnp.max(scores[j], axis=1, keepdims=True))
    denominator = jnp.zeros_like(top)
    numerator = jnp.zeros((rows * heads, head), jnp.float32)
    for j in range(slots):
        weights = jnp.exp(scores[j] - top).astype(jnp.bfloat16)
        denominator += jnp.sum(weights.astype(jnp.float32), axis=1, keepdims=True)
        numerator += jnp.dot(weights, values[j], preferred_element_type=jnp.float32)
    factor = jnp.where(live, gate[0], 0.0)
    attended = (numerator / denominator * factor).astype(out.dtype)
    for h in range(heads):
        out[:, h * head : (h + 1) * head] = attended[h * rows : (h + 1) * rows]


def attention(core, owners, counts, gate_value, query, near, far, q_gain, pieces):
    blocks = owners.shape[0]
    tokens, width = query.shape
    rows = tokens // blocks
    return pl.pallas_call(
        attention_kernel,
        grid=(blocks,),
        in_specs=[
            *(scalar,) * 4,
            pl.BlockSpec((rows, width), lambda b: (b, 0)),
            whole(near.shape),
            whole(far.shape),
            whole(q_gain.shape),
            *(whole(p.shape) for p in pieces),
        ],
        out_specs=pl.BlockSpec((rows, width), lambda b: (b, 0)),
        out_shape=jax.ShapeDtypeStruct((tokens, width), jnp.bfloat16),
        name="attention",
    )(core, owners, counts, gate_value, query, near, far, q_gain, *pieces)


def on_device(
    text_states,
    text_gain,
    vision,
    q_weight,
    k_weight,
    v_weight,
    q_gain,
    k_gain,
    owners,
    counts,
    gate_value,
):
    head = q_gain.shape[0]
    tokens = vision.shape[1]
    width = text_states.shape[1]
    yl, co, x, z, yh = (lax.axis_size(a) for a in IMG + FSDP)
    place = lax.axis_index("x")
    core = lax.axis_index("co")

    high_y = lax.axis_index("yh")

    joined = join(k_weight, v_weight, q_weight)
    over = shift(joined, "yh", 1)
    far = shift(joined, "x", 2)
    both = lax.ppermute(
        joined,
        ("x", "yh"),
        [(i * yh + h, (i + 2) % x * yh + 1 - h) for i in range(x) for h in range(yh)],
    )
    near = pile((joined, over), 0, 2 * head)
    left = shift(near, "x", 1)
    right = shift(near, "x", 3)
    pair_weight = [
        (joined, 0),
        (over, 0),
        (left, 0),
        (left, 1),
        (far, 0),
        (both, 0),
        (right, 0),
        (right, 1),
    ]

    rows_q = pile((joined, over, far, both), 2 * head, joined.shape[1])
    q_half = lax.all_gather(rows_q, "z", axis=0, tiled=True)

    columns = columns_of(vision.reshape(tokens, width), yl, x, z)
    here = exchange(columns.reshape(yl * z, tokens, width // z), ("yl", "z"))

    gate = jnp.tanh(gate_value)

    gain = text_gain[None]

    def partner(array):
        return lax.ppermute(array, "x", [(i, i ^ 1) for i in range(x)])

    choice = jnp.stack((core, place, high_y)).astype(jnp.int32)
    text_half, sent = half_rows(text_states, gain, choice, None, x, z, yh)
    guest = partner(sent)
    guest_other = shift(guest, "co", 1)
    choice = jnp.stack((1 - core, place, high_y)).astype(jnp.int32)
    (text_half,) = half_rows(text_states, gain, choice, text_half, x, z, yh)

    there = shift(here, "co", 1)
    partial = partial_sums(
        here.reshape(yl * z * tokens, width // z),
        there.reshape(yl * z * tokens, width // z),
        jnp.stack((place, high_y)).astype(jnp.int32),
        pair_weight,
        2 * head,
        x,
        z,
        yl,
        tokens,
    )
    parts = exchange(partial, "z")
    odd = lax.axis_index("co").astype(jnp.int32)[None]
    pair = pairs_of(odd, parts, k_gain[None], z * yh)
    own = exchange(pair, ("z", "yh"))
    own = own.transpose(1, 0, 2, 3).reshape(yl * co, z * yh * tokens, 2 * head)
    after = shift(own, "x", 1)
    before = shift(own, "x", -1)
    half = yl * co // 2
    low = shift(after[:half], "x", 1)
    high = shift(before[half:], "x", -1)

    guest_near = jnp.dot(guest, q_half, preferred_element_type=jnp.float32)
    guest_far = jnp.dot(guest_other, q_half, preferred_element_type=jnp.float32)
    back_near = partner(guest_near)
    back_far = partner(guest_far)
    query = jnp.dot(text_half, q_half, preferred_element_type=jnp.float32)
    return attention(
        core.astype(jnp.int32)[None],
        owners,
        counts,
        gate,
        query,
        back_near,
        back_far,
        q_gain[None],
        (own, after, before, low, high),
    )


def solution(mesh):
    fine = Mesh(mesh.devices.reshape(SIZES), IMG + FSDP)
    in_specs = (
        P(FSDP, None),
        P(),
        P(IMG, FSDP, None),
        P(FSDP, IMG),
        P(FSDP, IMG),
        P(FSDP, IMG),
        P(),
        P(),
        P(FSDP, None),
        P(FSDP),
        P(),
    )
    return jax.shard_map(
        on_device, mesh=fine, in_specs=in_specs, out_specs=P(FSDP, IMG), check_vma=False
    )
```

```python
import functools

import jax
import jax.numpy as jnp
from jax import lax
from jax.experimental import pallas as pl
from jax.experimental.pallas import tpu as pltpu
from jax.sharding import Mesh, PartitionSpec as P


norm_epsilon = 1e-05
masked_score = -1e30


IMG = ("yl", "co")
FSDP = ("x", "z", "yh")
SIZES = (4, 2, 4, 8, 2)


def shift(array, axis, step):
    size = lax.axis_size(axis)
    return lax.ppermute(array, axis, [(i, (i + step) % size) for i in range(size)])


def exchange(array, axes):
    return lax.all_to_all(array, axes, 0, 0, tiled=True)


def head_norm(values, gain):
    mean_square = jnp.mean(values * values, axis=-1, keepdims=True)
    return values * lax.rsqrt(mean_square + norm_epsilon) * gain


def whole(shape):
    return pl.BlockSpec(shape, lambda *_: (0,) * len(shape))


scalar = pl.BlockSpec(memory_space=pltpu.SMEM)


def half_kernel(x, z, choice, states, gain, *rest):
    outs = rest[1:]
    rows, width = states.shape
    depth = 128
    span = width // (x * z)
    squares = jnp.zeros((rows, depth), jnp.float32)
    for j in range(width // depth):
        wide = states[:, j * depth : (j + 1) * depth].astype(jnp.float32)
        squares += wide * wide
    scale = lax.rsqrt(jnp.sum(squares, axis=-1, keepdims=True) / width + norm_epsilon)
    even = choice[1] == 0
    for k in range(z):
        for m in range(x // 2):
            blocks = []
            for p in range(2):
                start = ((2 * m + p) * z + k) * span
                at = slice(start, start + span)
                wide = states[:, at].astype(jnp.float32)
                blocks.append((wide * scale * gain[:, at]).astype(jnp.bfloat16))
            start = (k * (x // 2) + m) * span
            lanes = slice(start, start + span)
            outs[0][:, lanes] = jnp.where(even, blocks[0], blocks[1])
            if len(outs) > 1:
                outs[1][:, lanes] = jnp.where(even, blocks[1], blocks[0])


def half_rows(states, gain, choice, base, x, z):
    total, width = states.shape
    rows = 32
    steps = total // 2 // rows
    held = () if base is None else (base,)
    place = pl.BlockSpec((rows, width // 2), lambda i, c: (c[0] * steps + i, 0))
    shapes = [jax.ShapeDtypeStruct((total, width // 2), jnp.bfloat16)]
    places = [place]
    if base is None:
        held = (gain,)
        shapes.append(jax.ShapeDtypeStruct((total // 2, width // 2), jnp.bfloat16))
        places.append(pl.BlockSpec((rows, width // 2), lambda i, c: (i, 0)))
    return pl.pallas_call(
        functools.partial(half_kernel, x, z),
        grid_spec=pltpu.PrefetchScalarGridSpec(
            num_scalar_prefetch=1,
            grid=(steps,),
            in_specs=[
                pl.BlockSpec((rows, width), lambda i, c: (c[0] * steps + i, 0)),
                pl.BlockSpec((1, width), lambda i, c: (0, 0)),
                pl.BlockSpec(memory_space=pl.ANY),
            ],
            out_specs=places,
        ),
        out_shape=shapes,
        input_output_aliases={} if base is None else {3: 0},
        name="half_rows",
    )(choice, states, gain, *held)


def join_kernel(*refs):
    *parts, out = refs
    start = 0
    for part in parts:
        width = part.shape[1]
        out[:, start : start + width] = part[...]
        start += width


def join(*parts):
    shape = (parts[0].shape[0], sum(p.shape[1] for p in parts))
    return pl.pallas_call(
        join_kernel,
        in_specs=[whole(p.shape) for p in parts],
        out_specs=whole(shape),
        grid=(1,),
        out_shape=jax.ShapeDtypeStruct(shape, parts[0].dtype),
        name="join",
    )(*parts)


def columns_kernel(x, vision, out):
    copies, z, _, width = out.shape
    span = width // x
    for c in range(copies):
        for k in range(z):
            for j in range(x):
                start = (j * z + k) * span
                out[c, k, :, j * span : (j + 1) * span] = vision[:, start : start + span]


def columns_of(vision, copies, x, z):
    tokens, width = vision.shape
    shape = (copies, z, tokens, width // z)
    return pl.pallas_call(
        functools.partial(columns_kernel, x),
        in_specs=[whole(vision.shape)],
        out_specs=whole(shape),
        grid=(1,),
        out_shape=jax.ShapeDtypeStruct(shape, vision.dtype),
        name="columns",
    )(vision)


def partial_kernel(spot, here, there, *rest):
    *weights, out = rest
    z, _, yl, tokens, width = out.shape
    x = len(weights)
    span = weights[0].shape[0]
    for c, part in enumerate((here, there)):
        product = jnp.zeros((part.shape[0], width), jnp.float32)
        for k, weight in enumerate(weights):
            start = pl.multiple_of(lax.rem(spot[0] + x - k, x) * span, span)
            product += jnp.dot(
                part[:, pl.ds(start, span)], weight[...], preferred_element_type=jnp.float32
            )
        for a in range(yl):
            for k in range(z):
                row = (a * z + k) * tokens
                out[k, c, a] = product[row : row + tokens]


def partial_sums(here, there, spot, weights, width, z, yl, tokens):
    shape = (z, 2, yl, tokens, width)
    return pl.pallas_call(
        partial_kernel,
        in_specs=[
            scalar,
            whole(here.shape),
            whole(there.shape),
            *(whole((w.shape[0], width)) for w in weights),
        ],
        out_specs=whole(shape),
        grid=(1,),
        out_shape=jax.ShapeDtypeStruct(shape, jnp.float32),
        name="partial_sums",
    )(spot, here, there, *weights)


def pair_kernel(odd, parts, k_gain, out):
    sources, cores, yl, tokens, width = parts.shape
    head = width // 2
    copies = out.shape[0]
    swap = odd[0] != 0
    total = parts[0]
    for s in range(1, sources):
        total = total + parts[s]
    rows = jnp.concatenate([total[c, a] for c in range(cores) for a in range(yl)], axis=0)
    keys = head_norm(rows[:, :head], k_gain[...]).astype(out.dtype)
    values = rows[:, head:].astype(out.dtype)
    half = yl * tokens
    for a in range(yl):
        near = slice(a * tokens, (a + 1) * tokens)
        far = slice(half + a * tokens, half + (a + 1) * tokens)
        for piece, lanes in ((keys, slice(0, head)), (values, slice(head, width))):
            even_core = jnp.where(swap, piece[far], piece[near])
            odd_core = jnp.where(swap, piece[near], piece[far])
            for c in range(copies):
                out[c, 2 * a, :, lanes] = even_core
                out[c, 2 * a + 1, :, lanes] = odd_core


def pairs_of(odd, parts, k_gain, copies):
    _, cores, yl, tokens, width = parts.shape
    shape = (copies, cores * yl, tokens, width)
    return pl.pallas_call(
        pair_kernel,
        in_specs=[scalar, whole(parts.shape), whole(k_gain.shape)],
        out_specs=whole(shape),
        grid=(1,),
        out_shape=jax.ShapeDtypeStruct(shape, jnp.bfloat16),
        name="key_value_pairs",
    )(odd, parts, k_gain)


def attention_kernel(
    core, owners, counts, gate, query, near, far, q_gain, *rest
):
    *pieces, out = rest
    block = pl.program_id(0)
    rows, width = query.shape
    images = pieces[0].shape[0]
    head = q_gain.shape[1]
    heads = width // head
    slots = owners.shape[1]
    scale = head ** (-0.5)
    gain = q_gain[...]
    span = near.shape[0]
    first = block * rows
    inside = lax.rem(first, span)
    at = pl.ds(pl.multiple_of(inside, rows), rows)
    total = query[...] + jnp.where(first // span == core[0], near[at, :], far[at, :])
    parts = []
    for h in range(heads):
        parts.append(head_norm(total[:, h * head : (h + 1) * head], gain).astype(jnp.bfloat16))
    queries = jnp.concatenate(parts, axis=0)
    count = counts[block]
    names = [owners[block, j] for j in range(slots)]
    scores = []
    values = []
    live = jnp.bool_(False)
    for j in range(slots):
        valid = j < count
        for i in range(j):
            valid = valid & (names[i] != names[j])
        live = live | valid
        image = jnp.clip(names[j], 0, images - 1)
        pairs = jnp.concatenate([piece[image] for piece in pieces], axis=0)
        values.append(pairs[:, head:])
        score = (
            lax.dot_general(
                queries, pairs[:, :head], (((1,), (1,)), ((), ())), preferred_element_type=jnp.float32
            )
            * scale
        )
        scores.append(jnp.where(valid, score, masked_score))
    top = jnp.max(scores[0], axis=1, keepdims=True)
    for j in range(1, slots):
        top = jnp.maximum(top, jnp.max(scores[j], axis=1, keepdims=True))
    denominator = jnp.zeros_like(top)
    numerator = jnp.zeros((rows * heads, head), jnp.float32)
    for j in range(slots):
        weights = jnp.exp(scores[j] - top).astype(jnp.bfloat16)
        denominator += jnp.sum(weights.astype(jnp.float32), axis=1, keepdims=True)
        numerator += jnp.dot(weights, values[j], preferred_element_type=jnp.float32)
    factor = jnp.where(live, gate[0], 0.0)
    attended = (numerator / denominator * factor).astype(out.dtype)
    for h in range(heads):
        out[:, h * head : (h + 1) * head] = attended[h * rows : (h + 1) * rows]


def attention(core, owners, counts, gate_value, query, near, far, q_gain, pieces):
    blocks = owners.shape[0]
    tokens, width = query.shape
    rows = tokens // blocks
    return pl.pallas_call(
        attention_kernel,
        grid=(blocks,),
        in_specs=[
            *(scalar,) * 4,
            pl.BlockSpec((rows, width), lambda b: (b, 0)),
            whole(near.shape),
            whole(far.shape),
            whole(q_gain.shape),
            *(whole(p.shape) for p in pieces),
        ],
        out_specs=pl.BlockSpec((rows, width), lambda b: (b, 0)),
        out_shape=jax.ShapeDtypeStruct((tokens, width), jnp.bfloat16),
        name="attention",
    )(core, owners, counts, gate_value, query, near, far, q_gain, *pieces)


def on_device(
    text_states,
    text_gain,
    vision,
    q_weight,
    k_weight,
    v_weight,
    q_gain,
    k_gain,
    owners,
    counts,
    gate_value,
):
    head = q_gain.shape[0]
    tokens = vision.shape[1]
    width = text_states.shape[1]
    yl, co, x, z, yh = (lax.axis_size(a) for a in IMG + FSDP)
    place = lax.axis_index("x")
    core = lax.axis_index("co")

    def ordered(early, mine, other):
        return jnp.where(
            early,
            jnp.concatenate((mine, other), axis=0),
            jnp.concatenate((other, mine), axis=0),
        )

    joined = join(k_weight, v_weight, q_weight)
    other = shift(joined, "yh", 1)
    both = ordered(lax.axis_index("yh") == 0, joined, other)
    far = shift(both, "x", 2)
    near = both[:, : 2 * head]
    pair_weight = (both, shift(near, "x", 1), far, shift(near, "x", 3))

    rows_q = ordered(place < 2, both[:, 2 * head :], far[:, 2 * head :])
    q_half = lax.all_gather(rows_q, "z", axis=0, tiled=True)

    columns = columns_of(vision.reshape(tokens, width), yl, x, z)
    here = exchange(columns.reshape(yl * z, tokens, width // z), ("yl", "z"))

    gate = jnp.tanh(gate_value)

    mine = lax.rem(place, 2)
    gain = text_gain[None]

    def partner(array):
        return lax.ppermute(array, "x", [(i, i ^ 1) for i in range(x)])

    choice = jnp.stack((core, mine)).astype(jnp.int32)
    text_half, sent = half_rows(text_states, gain, choice, None, x, z)
    guest = partner(sent)
    guest_other = shift(guest, "co", 1)
    choice = jnp.stack((1 - core, mine)).astype(jnp.int32)
    (text_half,) = half_rows(text_states, gain, choice, text_half, x, z)

    there = shift(here, "co", 1)
    partial = partial_sums(
        here.reshape(yl * z * tokens, width // z),
        there.reshape(yl * z * tokens, width // z),
        place.astype(jnp.int32)[None],
        pair_weight,
        2 * head,
        z,
        yl,
        tokens,
    )
    parts = exchange(partial, "z")
    odd = lax.axis_index("co").astype(jnp.int32)[None]
    pair = pairs_of(odd, parts, k_gain[None], z * yh)
    own = exchange(pair, ("z", "yh"))
    own = own.transpose(1, 0, 2, 3).reshape(yl * co, z * yh * tokens, 2 * head)
    pieces = [own, *(shift(own, "x", k) for k in range(1, x))]

    guest_near = jnp.dot(guest, q_half, preferred_element_type=jnp.float32)
    guest_far = jnp.dot(guest_other, q_half, preferred_element_type=jnp.float32)
    back_near = partner(guest_near)
    back_far = partner(guest_far)
    query = jnp.dot(text_half, q_half, preferred_element_type=jnp.float32)
    return attention(
        core.astype(jnp.int32)[None],
        owners,
        counts,
        gate,
        query,
        back_near,
        back_far,
        q_gain[None],
        pieces,
    )


def solution(mesh):
    fine = Mesh(mesh.devices.reshape(SIZES), IMG + FSDP)
    in_specs = (
        P(FSDP, None),
        P(),
        P(IMG, FSDP, None),
        P(FSDP, IMG),
        P(FSDP, IMG),
        P(FSDP, IMG),
        P(),
        P(),
        P(FSDP, None),
        P(FSDP),
        P(),
    )
    return jax.shard_map(
        on_device, mesh=fine, in_specs=in_specs, out_specs=P(FSDP, IMG), check_vma=False
    )
```

```python
import functools

import jax
import jax.numpy as jnp
from jax import lax
from jax.experimental import pallas as pl
from jax.experimental.pallas import tpu as pltpu
from jax.sharding import Mesh, PartitionSpec as P


norm_epsilon = 1e-05
masked_score = -1e30


IMG = ("yl", "co")
FSDP = ("x", "z", "yh")
SIZES = (4, 2, 4, 8, 2)


def shift(array, axis, step):
    size = lax.axis_size(axis)
    return lax.ppermute(array, axis, [(i, (i + step) % size) for i in range(size)])


def exchange(array, axes):
    return lax.all_to_all(array, axes, 0, 0, tiled=True)


def head_norm(values, gain):
    mean_square = jnp.mean(values * values, axis=-1, keepdims=True)
    return values * lax.rsqrt(mean_square + norm_epsilon) * gain


def near_core(*arrays):
    return [pltpu.with_memory_space_constraint(array, pltpu.VMEM) for array in arrays]


def whole(shape):
    return pl.BlockSpec(shape, lambda *_: (0,) * len(shape))


scalar = pl.BlockSpec(memory_space=pltpu.SMEM)
resident = pl.BlockSpec(memory_space=pltpu.VMEM)


def half_kernel(x, z, choice, states, gain, *rest):
    outs = rest[1:]
    rows, width = states.shape
    depth = 128
    span = width // (x * z)
    squares = jnp.zeros((rows, depth), jnp.float32)
    for j in range(width // depth):
        wide = states[:, j * depth : (j + 1) * depth].astype(jnp.float32)
        squares += wide * wide
    scale = lax.rsqrt(jnp.sum(squares, axis=-1, keepdims=True) / width + norm_epsilon)
    even = choice[1] == 0
    for k in range(z):
        for m in range(x // 2):
            blocks = []
            for p in range(2):
                start = ((2 * m + p) * z + k) * span
                at = slice(start, start + span)
                wide = states[:, at].astype(jnp.float32)
                blocks.append((wide * scale * gain[:, at]).astype(jnp.bfloat16))
            start = (k * (x // 2) + m) * span
            lanes = slice(start, start + span)
            outs[0][:, lanes] = jnp.where(even, blocks[0], blocks[1])
            if len(outs) > 1:
                outs[1][:, lanes] = jnp.where(even, blocks[1], blocks[0])


def half_rows(states, gain, choice, base, x, z):
    total, width = states.shape
    rows = 32
    steps = total // 2 // rows
    held = () if base is None else (base,)
    place = pl.BlockSpec((rows, width // 2), lambda i, c: (c[0] * steps + i, 0))
    shapes = [jax.ShapeDtypeStruct((total, width // 2), jnp.bfloat16)]
    places = [place]
    if base is None:
        held = (gain,)
        shapes.append(jax.ShapeDtypeStruct((total // 2, width // 2), jnp.bfloat16))
        places.append(pl.BlockSpec((rows, width // 2), lambda i, c: (i, 0)))
    return pl.pallas_call(
        functools.partial(half_kernel, x, z),
        grid_spec=pltpu.PrefetchScalarGridSpec(
            num_scalar_prefetch=1,
            grid=(steps,),
            in_specs=[
                pl.BlockSpec((rows, width), lambda i, c: (c[0] * steps + i, 0)),
                pl.BlockSpec((1, width), lambda i, c: (0, 0)),
                pl.BlockSpec(memory_space=pl.ANY),
            ],
            out_specs=places,
        ),
        out_shape=shapes,
        input_output_aliases={} if base is None else {3: 0},
        name="half_rows",
    )(choice, states, gain, *held)


def join_kernel(*refs):
    *parts, out = refs
    start = 0
    for part in parts:
        width = part.shape[1]
        out[:, start : start + width] = part[...]
        start += width


def join(*parts):
    shape = (parts[0].shape[0], sum(p.shape[1] for p in parts))
    return pl.pallas_call(
        join_kernel,
        in_specs=[whole(p.shape) for p in parts],
        out_specs=whole(shape),
        grid=(1,),
        out_shape=jax.ShapeDtypeStruct(shape, parts[0].dtype),
        name="join",
    )(*parts)


def columns_kernel(x, vision, out):
    copies, z, _, width = out.shape
    span = width // x
    for c in range(copies):
        for k in range(z):
            for j in range(x):
                start = (j * z + k) * span
                out[c, k, :, j * span : (j + 1) * span] = vision[:, start : start + span]


def columns_of(vision, copies, x, z):
    tokens, width = vision.shape
    shape = (copies, z, tokens, width // z)
    return pl.pallas_call(
        functools.partial(columns_kernel, x),
        in_specs=[whole(vision.shape)],
        out_specs=whole(shape),
        grid=(1,),
        out_shape=jax.ShapeDtypeStruct(shape, vision.dtype),
        name="columns",
    )(vision)


def partial_kernel(here, there, *rest):
    *weights, out = rest
    z, _, yl, tokens, width = out.shape
    x = len(weights)
    span = weights[0].shape[0]
    for c, part in enumerate((here, there)):
        product = jnp.zeros((part.shape[0], width), jnp.float32)
        for k, weight in enumerate(weights):
            start = pl.multiple_of(lax.rem(lax.axis_index("x") + x - k, x) * span, span)
            product += jnp.dot(
                part[:, pl.ds(start, span)], weight[...], preferred_element_type=jnp.float32
            )
        for a in range(yl):
            for k in range(z):
                row = (a * z + k) * tokens
                out[k, c, a] = product[row : row + tokens]


def partial_sums(here, there, weights, width, z, yl, tokens):
    shape = (z, 2, yl, tokens, width)
    return pl.pallas_call(
        partial_kernel,
        in_specs=[
            resident,
            resident,
            *(whole((w.shape[0], width)) for w in weights),
        ],
        out_specs=whole(shape),
        grid=(1,),
        out_shape=jax.ShapeDtypeStruct(shape, jnp.float32),
        name="partial_sums",
    )(*near_core(here, there), *weights)


def pair_kernel(parts, k_gain, out):
    sources, cores, yl, tokens, width = parts.shape
    head = width // 2
    copies = out.shape[0]
    swap = lax.axis_index("co") != 0
    total = parts[0]
    for s in range(1, sources):
        total = total + parts[s]
    rows = jnp.concatenate([total[c, a] for c in range(cores) for a in range(yl)], axis=0)
    keys = head_norm(rows[:, :head], k_gain[...]).astype(out.dtype)
    values = rows[:, head:].astype(out.dtype)
    half = yl * tokens
    for a in range(yl):
        near = slice(a * tokens, (a + 1) * tokens)
        far = slice(half + a * tokens, half + (a + 1) * tokens)
        for piece, lanes in ((keys, slice(0, head)), (values, slice(head, width))):
            even_core = jnp.where(swap, piece[far], piece[near])
            odd_core = jnp.where(swap, piece[near], piece[far])
            for c in range(copies):
                out[c, 2 * a, :, lanes] = even_core
                out[c, 2 * a + 1, :, lanes] = odd_core


def pairs_of(parts, k_gain, copies):
    _, cores, yl, tokens, width = parts.shape
    shape = (copies, cores * yl, tokens, width)
    return pl.pallas_call(
        pair_kernel,
        in_specs=[resident, whole(k_gain.shape)],
        out_specs=whole(shape),
        grid=(1,),
        out_shape=jax.ShapeDtypeStruct(shape, jnp.bfloat16),
        name="key_value_pairs",
    )(*near_core(parts), k_gain)


def attention_kernel(
    owners, counts, gate, query, near, far, q_gain, *rest
):
    *pieces, out = rest
    block = pl.program_id(0)
    rows, width = query.shape
    images = pieces[0].shape[0]
    head = q_gain.shape[1]
    heads = width // head
    slots = owners.shape[1]
    scale = head ** (-0.5)
    gain = q_gain[...]
    span = near.shape[0]
    first = block * rows
    inside = lax.rem(first, span)
    at = pl.ds(pl.multiple_of(inside, rows), rows)
    total = query[...] + jnp.where(first // span == lax.axis_index("co"), near[at, :], far[at, :])
    parts = []
    for h in range(heads):
        parts.append(head_norm(total[:, h * head : (h + 1) * head], gain).astype(jnp.bfloat16))
    queries = jnp.concatenate(parts, axis=0)
    count = counts[block]
    names = [owners[block, j] for j in range(slots)]
    scores = []
    values = []
    live = jnp.bool_(False)
    for j in range(slots):
        valid = j < count
        for i in range(j):
            valid = valid & (names[i] != names[j])
        live = live | valid
        image = jnp.clip(names[j], 0, images - 1)
        pairs = jnp.concatenate([piece[image] for piece in pieces], axis=0)
        values.append(pairs[:, head:])
        score = (
            lax.dot_general(
                queries, pairs[:, :head], (((1,), (1,)), ((), ())), preferred_element_type=jnp.float32
            )
            * scale
        )
        scores.append(jnp.where(valid, score, masked_score))
    top = jnp.max(scores[0], axis=1, keepdims=True)
    for j in range(1, slots):
        top = jnp.maximum(top, jnp.max(scores[j], axis=1, keepdims=True))
    denominator = jnp.zeros_like(top)
    numerator = jnp.zeros((rows * heads, head), jnp.float32)
    for j in range(slots):
        weights = jnp.exp(scores[j] - top).astype(jnp.bfloat16)
        denominator += jnp.sum(weights.astype(jnp.float32), axis=1, keepdims=True)
        numerator += jnp.dot(weights, values[j], preferred_element_type=jnp.float32)
    factor = jnp.where(live, gate[0], 0.0)
    attended = (numerator / denominator * factor).astype(out.dtype)
    for h in range(heads):
        out[:, h * head : (h + 1) * head] = attended[h * rows : (h + 1) * rows]


def attention(owners, counts, gate_value, query, near, far, q_gain, pieces):
    blocks = owners.shape[0]
    tokens, width = query.shape
    rows = tokens // blocks
    return pl.pallas_call(
        attention_kernel,
        grid=(blocks,),
        in_specs=[
            *(scalar,) * 3,
            pl.BlockSpec((rows, width), lambda b: (b, 0)),
            resident,
            resident,
            whole(q_gain.shape),
            *(resident for _ in pieces),
        ],
        out_specs=pl.BlockSpec((rows, width), lambda b: (b, 0)),
        out_shape=jax.ShapeDtypeStruct((tokens, width), jnp.bfloat16),
        name="attention",
    )(owners, counts, gate_value, query, *near_core(near, far), q_gain, *near_core(*pieces))


def on_device(
    text_states,
    text_gain,
    vision,
    q_weight,
    k_weight,
    v_weight,
    q_gain,
    k_gain,
    owners,
    counts,
    gate_value,
):
    head = q_gain.shape[0]
    tokens = vision.shape[1]
    width = text_states.shape[1]
    yl, co, x, z, yh = (lax.axis_size(a) for a in IMG + FSDP)
    place = lax.axis_index("x")
    core = lax.axis_index("co")

    def ordered(early, mine, other):
        return jnp.where(
            early,
            jnp.concatenate((mine, other), axis=0),
            jnp.concatenate((other, mine), axis=0),
        )

    joined = join(k_weight, v_weight, q_weight)
    other = shift(joined, "yh", 1)
    both = ordered(lax.axis_index("yh") == 0, joined, other)
    far = shift(both, "x", 2)
    near = both[:, : 2 * head]
    pair_weight = (both, shift(near, "x", 1), far, shift(near, "x", 3))

    rows_q = ordered(place < 2, both[:, 2 * head :], far[:, 2 * head :])
    q_half = lax.all_gather(rows_q, "z", axis=0, tiled=True)

    columns = columns_of(vision.reshape(tokens, width), yl, x, z)
    here = exchange(columns.reshape(yl * z, tokens, width // z), ("yl", "z"))

    gate = jnp.tanh(gate_value)

    mine = lax.rem(place, 2)
    gain = text_gain[None]

    def partner(array):
        return lax.ppermute(array, "x", [(i, i ^ 1) for i in range(x)])

    choice = jnp.stack((core, mine)).astype(jnp.int32)
    text_half, sent = half_rows(text_states, gain, choice, None, x, z)
    guest = partner(sent)
    guest_other = shift(guest, "co", 1)
    choice = jnp.stack((1 - core, mine)).astype(jnp.int32)
    (text_half,) = half_rows(text_states, gain, choice, text_half, x, z)

    there = shift(here, "co", 1)
    partial = partial_sums(
        here.reshape(yl * z * tokens, width // z),
        there.reshape(yl * z * tokens, width // z),
        pair_weight,
        2 * head,
        z,
        yl,
        tokens,
    )
    parts = exchange(partial, "z")
    pair = pairs_of(parts, k_gain[None], z * yh)
    own = exchange(pair, ("z", "yh"))
    own = own.transpose(1, 0, 2, 3).reshape(yl * co, z * yh * tokens, 2 * head)
    pieces = [own, *(shift(own, "x", k) for k in range(1, x))]

    guest_near = jnp.dot(guest, q_half, preferred_element_type=jnp.float32)
    guest_far = jnp.dot(guest_other, q_half, preferred_element_type=jnp.float32)
    back_near = partner(guest_near)
    back_far = partner(guest_far)
    query = jnp.dot(text_half, q_half, preferred_element_type=jnp.float32)
    return attention(
        owners,
        counts,
        gate,
        query,
        back_near,
        back_far,
        q_gain[None],
        pieces,
    )


def solution(mesh):
    fine = Mesh(mesh.devices.reshape(SIZES), IMG + FSDP)
    in_specs = (
        P(FSDP, None),
        P(),
        P(IMG, FSDP, None),
        P(FSDP, IMG),
        P(FSDP, IMG),
        P(FSDP, IMG),
        P(),
        P(),
        P(FSDP, None),
        P(FSDP),
        P(),
    )
    return jax.shard_map(
        on_device, mesh=fine, in_specs=in_specs, out_specs=P(FSDP, IMG), check_vma=False
    )
```

```python
import functools

import jax
import jax.numpy as jnp
from jax import lax
from jax.experimental import pallas as pl
from jax.experimental.pallas import tpu as pltpu
from jax.sharding import Mesh, PartitionSpec as P


norm_epsilon = 1e-05
masked_score = -1e30


IMG = ("yl", "co")
FSDP = ("x", "z", "yh")
SIZES = (4, 2, 4, 8, 2)


def shift(array, axis, step):
    size = lax.axis_size(axis)
    return lax.ppermute(array, axis, [(i, (i + step) % size) for i in range(size)])


def exchange(array, axes):
    return lax.all_to_all(array, axes, 0, 0, tiled=True)


def head_norm(values, gain):
    mean_square = jnp.mean(values * values, axis=-1, keepdims=True)
    return values * lax.rsqrt(mean_square + norm_epsilon) * gain


def near_core(*arrays):
    return [pltpu.with_memory_space_constraint(array, pltpu.VMEM) for array in arrays]


def whole(shape):
    return pl.BlockSpec(shape, lambda *_: (0,) * len(shape))


scalar = pl.BlockSpec(memory_space=pltpu.SMEM)
resident = pl.BlockSpec(memory_space=pltpu.VMEM)


def half_kernel(x, z, choice, states, gain, *rest):
    outs = rest[1:]
    rows, width = states.shape
    depth = 128
    span = width // (x * z)
    squares = jnp.zeros((rows, depth), jnp.float32)
    for j in range(width // depth):
        wide = states[:, j * depth : (j + 1) * depth].astype(jnp.float32)
        squares += wide * wide
    scale = lax.rsqrt(jnp.sum(squares, axis=-1, keepdims=True) / width + norm_epsilon)
    quarter = width // x
    for index, out in enumerate(outs):
        home = choice[1] if index == 0 else choice[1] + 1 - 2 * lax.rem(choice[1], 2)
        for m in range(x // 2):
            first = lax.rem(home + 2 * m, x) * quarter
            for k in range(z):
                at = pl.ds(pl.multiple_of(first + k * span, span), span)
                wide = states[:, at].astype(jnp.float32)
                start = m * quarter + k * span
                out[:, start : start + span] = (wide * scale * gain[:, at]).astype(out.dtype)


def half_rows(states, gain, choice, base, x, z):
    total, width = states.shape
    rows = 32
    steps = total // 2 // rows
    held = () if base is None else (base,)
    place = pl.BlockSpec((rows, width // 2), lambda i, c: (c[0] * steps + i, 0))
    shapes = [jax.ShapeDtypeStruct((total, width // 2), jnp.bfloat16)]
    places = [place]
    if base is None:
        held = (gain,)
        shapes.append(jax.ShapeDtypeStruct((total // 2, width // 2), jnp.bfloat16))
        places.append(pl.BlockSpec((rows, width // 2), lambda i, c: (i, 0)))
    return pl.pallas_call(
        functools.partial(half_kernel, x, z),
        grid_spec=pltpu.PrefetchScalarGridSpec(
            num_scalar_prefetch=1,
            grid=(steps,),
            in_specs=[
                pl.BlockSpec((rows, width), lambda i, c: (c[0] * steps + i, 0)),
                pl.BlockSpec((1, width), lambda i, c: (0, 0)),
                pl.BlockSpec(memory_space=pl.ANY),
            ],
            out_specs=places,
        ),
        out_shape=shapes,
        input_output_aliases={} if base is None else {3: 0},
        name="half_rows",
    )(choice, states, gain, *held)


def join_kernel(*refs):
    *parts, out = refs
    start = 0
    for part in parts:
        width = part.shape[1]
        out[:, start : start + width] = part[...]
        start += width


def join(*parts):
    shape = (parts[0].shape[0], sum(p.shape[1] for p in parts))
    return pl.pallas_call(
        join_kernel,
        in_specs=[whole(p.shape) for p in parts],
        out_specs=whole(shape),
        grid=(1,),
        out_shape=jax.ShapeDtypeStruct(shape, parts[0].dtype),
        name="join",
    )(*parts)


def columns_kernel(x, vision, out):
    copies, z, _, width = out.shape
    span = width // x
    for c in range(copies):
        for k in range(z):
            for j in range(x):
                start = (j * z + k) * span
                out[c, k, :, j * span : (j + 1) * span] = vision[:, start : start + span]


def columns_of(vision, copies, x, z):
    tokens, width = vision.shape
    shape = (copies, z, tokens, width // z)
    return pl.pallas_call(
        functools.partial(columns_kernel, x),
        in_specs=[whole(vision.shape)],
        out_specs=whole(shape),
        grid=(1,),
        out_shape=jax.ShapeDtypeStruct(shape, vision.dtype),
        name="columns",
    )(vision)


def partial_kernel(here, there, *rest):
    *weights, out = rest
    z, _, yl, tokens, width = out.shape
    x = len(weights)
    span = weights[0].shape[0]
    for c, part in enumerate((here, there)):
        product = jnp.zeros((part.shape[0], width), jnp.float32)
        for k, weight in enumerate(weights):
            start = pl.multiple_of(lax.rem(lax.axis_index("x") + x - k, x) * span, span)
            product += jnp.dot(
                part[:, pl.ds(start, span)], weight[...], preferred_element_type=jnp.float32
            )
        for a in range(yl):
            for k in range(z):
                row = (a * z + k) * tokens
                out[k, c, a] = product[row : row + tokens]


def partial_sums(here, there, weights, width, z, yl, tokens):
    shape = (z, 2, yl, tokens, width)
    return pl.pallas_call(
        partial_kernel,
        in_specs=[
            resident,
            resident,
            *(whole((w.shape[0], width)) for w in weights),
        ],
        out_specs=whole(shape),
        grid=(1,),
        out_shape=jax.ShapeDtypeStruct(shape, jnp.float32),
        name="partial_sums",
    )(*near_core(here, there), *weights)


def pair_kernel(parts, k_gain, out):
    sources, cores, yl, tokens, width = parts.shape
    head = width // 2
    copies = out.shape[0]
    swap = lax.axis_index("co") != 0
    total = parts[0]
    for s in range(1, sources):
        total = total + parts[s]
    rows = jnp.concatenate([total[c, a] for c in range(cores) for a in range(yl)], axis=0)
    keys = head_norm(rows[:, :head], k_gain[...]).astype(out.dtype)
    values = rows[:, head:].astype(out.dtype)
    half = yl * tokens
    for a in range(yl):
        near = slice(a * tokens, (a + 1) * tokens)
        far = slice(half + a * tokens, half + (a + 1) * tokens)
        for piece, lanes in ((keys, slice(0, head)), (values, slice(head, width))):
            even_core = jnp.where(swap, piece[far], piece[near])
            odd_core = jnp.where(swap, piece[near], piece[far])
            for c in range(copies):
                out[c, 2 * a, :, lanes] = even_core
                out[c, 2 * a + 1, :, lanes] = odd_core


def pairs_of(parts, k_gain, copies):
    _, cores, yl, tokens, width = parts.shape
    shape = (copies, cores * yl, tokens, width)
    return pl.pallas_call(
        pair_kernel,
        in_specs=[resident, whole(k_gain.shape)],
        out_specs=whole(shape),
        grid=(1,),
        out_shape=jax.ShapeDtypeStruct(shape, jnp.bfloat16),
        name="key_value_pairs",
    )(*near_core(parts), k_gain)


def attention_kernel(
    owners, counts, gate, query, near, far, q_gain, *rest
):
    *pieces, out = rest
    block = pl.program_id(0)
    rows, width = query.shape
    images = pieces[0].shape[0]
    head = q_gain.shape[1]
    heads = width // head
    slots = owners.shape[1]
    scale = head ** (-0.5)
    gain = q_gain[...]
    span = near.shape[0]
    first = block * rows
    inside = lax.rem(first, span)
    at = pl.ds(pl.multiple_of(inside, rows), rows)
    total = query[...] + jnp.where(first // span == lax.axis_index("co"), near[at, :], far[at, :])
    parts = []
    for h in range(heads):
        parts.append(head_norm(total[:, h * head : (h + 1) * head], gain).astype(jnp.bfloat16))
    queries = jnp.concatenate(parts, axis=0)
    count = counts[block]
    names = [owners[block, j] for j in range(slots)]
    scores = []
    values = []
    live = jnp.bool_(False)
    for j in range(slots):
        valid = j < count
        for i in range(j):
            valid = valid & (names[i] != names[j])
        live = live | valid
        image = jnp.clip(names[j], 0, images - 1)
        pairs = jnp.concatenate([piece[image] for piece in pieces], axis=0)
        values.append(pairs[:, head:])
        score = (
            lax.dot_general(
                queries, pairs[:, :head], (((1,), (1,)), ((), ())), preferred_element_type=jnp.float32
            )
            * scale
        )
        scores.append(jnp.where(valid, score, masked_score))
    top = jnp.max(scores[0], axis=1, keepdims=True)
    for j in range(1, slots):
        top = jnp.maximum(top, jnp.max(scores[j], axis=1, keepdims=True))
    denominator = jnp.zeros_like(top)
    numerator = jnp.zeros((rows * heads, head), jnp.float32)
    for j in range(slots):
        weights = jnp.exp(scores[j] - top).astype(jnp.bfloat16)
        denominator += jnp.sum(weights.astype(jnp.float32), axis=1, keepdims=True)
        numerator += jnp.dot(weights, values[j], preferred_element_type=jnp.float32)
    factor = jnp.where(live, gate[0], 0.0)
    attended = (numerator / denominator * factor).astype(out.dtype)
    for h in range(heads):
        out[:, h * head : (h + 1) * head] = attended[h * rows : (h + 1) * rows]


def attention(owners, counts, gate_value, query, near, far, q_gain, pieces):
    blocks = owners.shape[0]
    tokens, width = query.shape
    rows = tokens // blocks
    return pl.pallas_call(
        attention_kernel,
        grid=(blocks,),
        in_specs=[
            *(scalar,) * 3,
            pl.BlockSpec((rows, width), lambda b: (b, 0)),
            resident,
            resident,
            whole(q_gain.shape),
            *(resident for _ in pieces),
        ],
        out_specs=pl.BlockSpec((rows, width), lambda b: (b, 0)),
        out_shape=jax.ShapeDtypeStruct((tokens, width), jnp.bfloat16),
        name="attention",
    )(owners, counts, gate_value, query, *near_core(near, far), q_gain, *near_core(*pieces))


def on_device(
    text_states,
    text_gain,
    vision,
    q_weight,
    k_weight,
    v_weight,
    q_gain,
    k_gain,
    owners,
    counts,
    gate_value,
):
    head = q_gain.shape[0]
    tokens = vision.shape[1]
    width = text_states.shape[1]
    yl, co, x, z, yh = (lax.axis_size(a) for a in IMG + FSDP)
    place = lax.axis_index("x")
    core = lax.axis_index("co")

    def ordered(early, mine, other):
        return jnp.where(
            early,
            jnp.concatenate((mine, other), axis=0),
            jnp.concatenate((other, mine), axis=0),
        )

    joined = join(k_weight, v_weight, q_weight)
    other = shift(joined, "yh", 1)
    both = ordered(lax.axis_index("yh") == 0, joined, other)
    far = shift(both, "x", 2)
    near = both[:, : 2 * head]
    pair_weight = (both, shift(near, "x", 1), far, shift(near, "x", 3))

    q_near = lax.all_gather(both[:, 2 * head :], "z", axis=0, tiled=True)
    q_far = lax.all_gather(far[:, 2 * head :], "z", axis=0, tiled=True)

    columns = columns_of(vision.reshape(tokens, width), yl, x, z)
    here = exchange(columns.reshape(yl * z, tokens, width // z), ("yl", "z"))

    gate = jnp.tanh(gate_value)

    gain = text_gain[None]

    def partner(array):
        return lax.ppermute(array, "x", [(i, i ^ 1) for i in range(x)])

    choice = jnp.stack((core, place)).astype(jnp.int32)
    text_half, sent = half_rows(text_states, gain, choice, None, x, z)
    guest = partner(sent)
    guest_other = shift(guest, "co", 1)
    choice = jnp.stack((1 - core, place)).astype(jnp.int32)
    (text_half,) = half_rows(text_states, gain, choice, text_half, x, z)

    there = shift(here, "co", 1)
    partial = partial_sums(
        here.reshape(yl * z * tokens, width // z),
        there.reshape(yl * z * tokens, width // z),
        pair_weight,
        2 * head,
        z,
        yl,
        tokens,
    )
    parts = exchange(partial, "z")
    pair = pairs_of(parts, k_gain[None], z * yh)
    own = exchange(pair, ("z", "yh"))
    own = own.transpose(1, 0, 2, 3).reshape(yl * co, z * yh * tokens, 2 * head)
    pieces = [own, *(shift(own, "x", k) for k in range(1, x))]

    def product(left, right):
        return jnp.dot(left, right, preferred_element_type=jnp.float32)

    cut = q_near.shape[0]
    guest_near_1 = product(guest[:, :cut], q_near)
    guest_far_1 = product(guest_other[:, :cut], q_near)
    query_1 = product(text_half[:, :cut], q_near)
    guest_near_1, guest_far_1, query_1 = lax.optimization_barrier(
        (guest_near_1, guest_far_1, query_1)
    )
    guest_near = guest_near_1 + product(guest[:, cut:], q_far)
    guest_far = guest_far_1 + product(guest_other[:, cut:], q_far)
    back_near = partner(guest_near)
    back_far = partner(guest_far)
    query = query_1 + product(text_half[:, cut:], q_far)
    return attention(
        owners,
        counts,
        gate,
        query,
        back_near,
        back_far,
        q_gain[None],
        pieces,
    )


def solution(mesh):
    fine = Mesh(mesh.devices.reshape(SIZES), IMG + FSDP)
    in_specs = (
        P(FSDP, None),
        P(),
        P(IMG, FSDP, None),
        P(FSDP, IMG),
        P(FSDP, IMG),
        P(FSDP, IMG),
        P(),
        P(),
        P(FSDP, None),
        P(FSDP),
        P(),
    )
    return jax.shard_map(
        on_device, mesh=fine, in_specs=in_specs, out_specs=P(FSDP, IMG), check_vma=False
    )
```
